256 devices in a mesh: tc: 128 (over z, x, y), pr: 2 (over core).
Axes of the slice: x: 4, y: 4, z: 8, core: 2. Of those that a mesh axis runs over, the one named last changes fastest.
Arguments:
- pivot_rhs: float32 [128, 1536, 64], P('tc', None, 'pr'), may hold values from -6 to 6
- pivot_inverse: bfloat16 [128, 1536, 1536], P('tc'), as said below
- pivot_owner: int32 [3], replicated, may hold values from 0 to 127, as said below
- coupling_left: bfloat16 [128, 2, 1536, 200], P('tc'), may hold values from -0.15625 to 0.15625
- coupling_right: bfloat16 [128, 2, 1536, 200], P('tc'), may hold values from -0.4375 to 0.4375
- coupling_ranks: int32 [128, 2], P('tc'), may hold values from 100 to 200, as said below
- future_left: bfloat16 [256, 3, 200, 1536], P('tc', None, None, 'pr'), may hold values from -0.15625 to 0.15625
- future_right: bfloat16 [256, 3, 200, 1536], P('tc', None, None, 'pr'), may hold values from -0.4375 to 0.4375
- future_ranks: int32 [256, 3], P('tc'), may hold values from 100 to 200, as said below
- future_rhs: float32 [256, 64, 1536], P('tc', None, 'pr'), may hold values from -6 to 6
Outputs:
- solved: bfloat16 [3, 1536, 64], P(None, None, 'pr')
- future_out: float32 [256, 64, 1536], P('tc', None, 'pr')
The draws below stay inside these ranges and needn't reach their ends.
Inputs may be any that keep to these rules, and one draw needn't show every extreme that they name: `pivot_owner`: the 3 entries are distinct; entry p names the slot, and so the index of tc, that holds pivot p's tiles. `coupling_ranks`: entry [s, j] is the rank of the tile from the pivot in slot s to the pivot j + 1 places later. In every draw a tile that the window uses has rank exactly 200. `future_ranks`: in every draw one of these tiles has rank exactly 200. `pivot_inverse`: each tile is lower triangular.
All inputs are finite; a program needn't handle non-finite values.
Results may differ from the reference program's by a relative error of at most 0.007.
Values may be sent and summed in bfloat16 or wider, within the bound.
A program may use at most 64 MiB of HBM per device.

```python
import math
import jax
import jax.numpy as jnp
from jax import lax

B = 1536
P_SIZE = 64
R = 200
PIV = 3
FUT = 256
SLOTS = 128


def draw_pivot_inverse(key, part):
    noise_key, diag_key = jax.random.split(jax.random.fold_in(key, 5))
    spread = jax.random.normal(noise_key, (SLOTS, B, B), jnp.float32) * (0.8 / math.sqrt(B))
    diagonal = jax.random.uniform(diag_key, (SLOTS, B), jnp.float32, 0.6, 1.6)
    rows = jnp.arange(B, dtype=jnp.int32)[:, None]
    columns = jnp.arange(B, dtype=jnp.int32)[None, :]
    below = jnp.where(rows > columns, spread, 0.0)
    return jnp.where(rows == columns, diagonal[:, :, None], below).astype(jnp.bfloat16)


def owner_slots(key):
    middle = jax.random.permutation(jax.random.fold_in(key, 21), SLOTS - 2)[:PIV - 2].astype(jnp.int32) + 1
    ends = jnp.array([0, SLOTS - 1], dtype=jnp.int32)
    values = jnp.concatenate([ends, middle])
    order = jax.random.permutation(jax.random.fold_in(key, 22), PIV)
    return values[order].astype(jnp.int32)


def draw_pivot_owner(key, part):
    return owner_slots(key)


def draw_coupling_ranks(key, part):
    owners = owner_slots(key)
    rank_values = jax.random.randint(jax.random.fold_in(key, 11), (SLOTS, PIV - 1), R // 2, R + 1, dtype=jnp.int32)
    return rank_values.at[owners[0], 0].set(R)


def draw_future_ranks(key, part):
    value_key, place_key = jax.random.split(jax.random.fold_in(key, 12))
    rank_values = jax.random.randint(value_key, (FUT * PIV,), R // 2, R + 1, dtype=jnp.int32)
    chosen = jax.random.randint(place_key, (), 0, FUT * PIV, dtype=jnp.int32)
    return rank_values.at[chosen].set(R).reshape(FUT, PIV)


def shard_levels(rng, extent, pieces, least, largest):
    loudness, own = 1.0, jax.random.fold_in(rng, 6)
    for position, blocks in pieces:
        draws = jnp.exp(jax.random.uniform(jax.random.fold_in(own, position), (blocks,), jnp.float32, least / len(pieces), largest / len(pieces)))
        loudness = loudness * jnp.repeat(draws, extent[position] // blocks).reshape([-1 if axis == position else 1 for axis in range(len(extent))])
    return loudness


def noise(key, shape, deviation, reach, cuts=(), kind=jnp.bfloat16):
    values = jax.random.normal(key, shape, jnp.float32) * deviation
    if len(cuts) > 0:
        values = shard_levels(key, shape, cuts, -0.22, 0.18) * values
    return jnp.clip(values, min=-reach, max=reach).astype(kind)


def setup_inputs(seed: int = 0) -> dict:
    keys = jax.random.split(jax.random.key(seed), 11)
    return {
        "pivot_rhs": noise(keys[0], (SLOTS, B, P_SIZE), 1.0, 6.0, ((0, 128), (2, 2)), jnp.float32),
        "pivot_inverse": draw_pivot_inverse(jax.random.fold_in(keys[10], 71), 0),
        "pivot_owner": draw_pivot_owner(jax.random.fold_in(keys[10], 71), 0),
        "coupling_left": noise(keys[3], (SLOTS, PIV - 1, B, R), B ** -0.5, 0.15625, ((0, 128),)),
        "coupling_right": noise(keys[4], (SLOTS, PIV - 1, B, R), R ** -0.5, 0.4375, ((0, 128),)),
        "coupling_ranks": draw_coupling_ranks(jax.random.fold_in(keys[10], 71), 0),
        "future_left": noise(keys[6], (FUT, PIV, R, B), B ** -0.5, 0.15625, ((0, 128), (3, 2))),
        "future_right": noise(keys[7], (FUT, PIV, R, B), R ** -0.5, 0.4375, ((0, 128), (3, 2))),
        "future_ranks": draw_future_ranks(jax.random.fold_in(keys[10], 71), 0),
        "future_rhs": noise(keys[9], (FUT, P_SIZE, B), 1.0, 6.0, ((0, 128), (2, 2)), jnp.float32),
    }


def reference(pivot_rhs, pivot_inverse, pivot_owner, coupling_left, coupling_right, coupling_ranks, future_left, future_right, future_ranks, future_rhs):
    rank_ids = jnp.arange(R, dtype=jnp.int32)
    pending = [pivot_rhs[pivot_owner[tile_id]] for tile_id in range(PIV)]
    solved = [None] * PIV
    for current in reversed(range(PIV)):
        pivot_in = pending[current].astype(jnp.bfloat16)
        solution = jnp.dot(pivot_inverse[pivot_owner[current]].T, pivot_in, preferred_element_type=jnp.float32).astype(jnp.bfloat16)
        solved[current] = solution
        for target in range(current - 1, -1, -1):
            slot_id = pivot_owner[target]
            entry_id = current - target - 1
            factor = jnp.dot(coupling_left[slot_id, entry_id].T, solution, preferred_element_type=jnp.float32)
            factor = jnp.where(rank_ids[:, None] < coupling_ranks[slot_id, entry_id], factor, 0.0).astype(jnp.bfloat16)
            pending[target] = pending[target] - jnp.dot(coupling_right[slot_id, entry_id], factor, preferred_element_type=jnp.float32)
    stacked = jnp.stack(solved)
    solved_wide = stacked.astype(jnp.float32)

    def one_tile(tile_args):
        left_tile, right_tile, tile_ranks, tile_rhs = tile_args
        weights = jnp.einsum("sbq,srb->sqr", solved_wide, left_tile.astype(jnp.float32))
        weights = jnp.where(rank_ids[None, None, :] < tile_ranks[:, None, None], weights, 0.0).astype(jnp.bfloat16)
        return tile_rhs - jnp.einsum("sqr,srb->qb", weights.astype(jnp.float32), right_tile.astype(jnp.float32))

    return stacked, lax.map(one_tile, (future_left, future_right, future_ranks, future_rhs))
```

```python
import functools

import jax
import jax.numpy as jnp
from jax import lax
from jax.experimental import pallas as pl
from jax.experimental.pallas import tpu as pltpu
from jax.sharding import Mesh
from jax.sharding import PartitionSpec as P

TC = ("tz", "tx", "ty")
MESH = pl.DeviceIdType.MESH
NZ, NX, NY, NC = 8, 4, 4, 2
PIV, B, PROBES, R = 3, 1536, 32, 200
GROUP, COLS = PROBES // NX, B // NY
BLOCK = 256


def ring_distance(step, size):
    return min(step, size - step)


PLANE = sorted(
    ((dx, dy) for dx in range(NX) for dy in range(NY) if (dx, dy) != (0, 0)),
    key=lambda d: -(ring_distance(d[0], NX) + ring_distance(d[1], NY)),
)
COLUMN = sorted(range(1, NZ), key=lambda d: -ring_distance(d, NZ))


def matmul(a, b):
    return lax.dot_general(a, b, (((1,), (0,)), ((), ())), preferred_element_type=jnp.float32)


def matmul_t(a, b):
    return lax.dot_general(a, b, (((1,), (1,)), ((), ())), preferred_element_type=jnp.float32)


def kernel(
    owner_ref, coupling_ranks_ref, future_ranks_ref,
    rhs_ref, inverse_ref, left_ref, right_ref, future_left_ref, future_right_ref, future_rhs_ref,
    solved_ref, future_out_ref,
    inverse, rhs, left, right, future_left, future_right, future, gain, acc, block,
    rs_send, rs_recv, z_send, z_recv, whole,
    load_sem, panel_sem, out_sem, swap_sem,
    rs_send_sem, rs_recv_sem, z_send_sem, z_recv_sem,
    own_send_sem, own_recv_sem, far_send_sem, far_recv_sem,
):
    mz, mx, my, mc = (lax.axis_index(name) for name in (*TC, "pr"))
    me = (mz * NX + mx) * NY + my
    other = 1 - mc

    def shifted(dx, dy):
        return lax.rem(mx + dx, NX), lax.rem(my + dy, NY)

    rhs_load = pltpu.make_async_copy(rhs_ref, rhs, load_sem.at[0])
    rhs_load.start()
    panels = []
    for k in range(B // BLOCK):
        rows, columns = pl.ds(k * BLOCK, BLOCK), pl.ds(0, (k + 1) * BLOCK)
        panel = pltpu.make_async_copy(
            inverse_ref.at[rows, columns], inverse.at[rows, columns], panel_sem.at[k]
        )
        panel.start()
        panels.append(panel)

    barrier = pltpu.get_barrier_semaphore()
    greeted = 0
    for dx, dy in PLANE:
        px, py = shifted(dx, dy)
        for core in (mc, other):
            pl.semaphore_signal(barrier, 1, device_id=(mz, px, py, core), device_id_type=MESH)
            greeted += 1
    for dz in COLUMN:
        pz = lax.rem(mz + dz, NZ)
        pl.semaphore_signal(barrier, 1, device_id=(pz, mx, my, mc), device_id_type=MESH)
        greeted += 1
    pl.semaphore_signal(barrier, 1, device_id=(mz, mx, my, other), device_id_type=MESH)
    greeted += 1

    loads = [
        pltpu.make_async_copy(right_ref, right, load_sem.at[1]),
        pltpu.make_async_copy(left_ref, left, load_sem.at[2]),
        pltpu.make_async_copy(future_left_ref, future_left.at[mc], load_sem.at[3]),
        pltpu.make_async_copy(future_right_ref, future_right, load_sem.at[4]),
        pltpu.make_async_copy(future_rhs_ref, future, load_sem.at[5]),
    ]

    rhs_load.wait()
    start = rhs[...].astype(jnp.bfloat16)
    sums = [None] * (B // BLOCK)
    for k in range(B // BLOCK):
        panels[k].wait()
        piece = start[:, k * BLOCK : (k + 1) * BLOCK]
        for c in range(k + 1):
            term = matmul(piece, inverse[k * BLOCK : (k + 1) * BLOCK, c * BLOCK : (c + 1) * BLOCK])
            sums[c] = term if sums[c] is None else sums[c] + term
    for c in range(B // BLOCK):
        acc[:, c * BLOCK : (c + 1) * BLOCK] = sums[c]
    for load in loads:
        load.start()
    pl.semaphore_wait(barrier, greeted)

    swap = pltpu.make_async_remote_copy(
        src_ref=future_left_ref,
        dst_ref=future_left.at[mc],
        send_sem=swap_sem.at[0],
        recv_sem=swap_sem.at[1],
        device_id=(mz, mx, my, other),
        device_id_type=MESH,
    )
    swap_in = pltpu.make_async_remote_copy(
        src_ref=future_left_ref,
        dst_ref=future_left.at[other],
        send_sem=swap_sem.at[0],
        recv_sem=swap_sem.at[1],
        device_id=(mz, mx, my, other),
        device_id_type=MESH,
    )

    own_pivot = jnp.int32(0)
    holds = jnp.int32(0)
    for p in range(PIV):
        mine = (owner_ref[p] == me).astype(jnp.int32)
        own_pivot = own_pivot + mine * p
        holds = holds + mine
    rank_ids = lax.broadcasted_iota(jnp.int32, (PROBES, R), 1)
    future_rank_ids = lax.broadcasted_iota(jnp.int32, (NC * PROBES, R), 1)

    sent = []

    def send(src, dst, send_sem, recv_sem, device):
        copy = pltpu.make_async_remote_copy(
            src_ref=src, dst_ref=dst, send_sem=send_sem, recv_sem=recv_sem,
            device_id=device, device_id_type=MESH,
        )
        copy.start()
        sent.append(copy)

    def receive(dst, send_sem, recv_sem):
        pltpu.make_async_remote_copy(
            src_ref=dst, dst_ref=dst, send_sem=send_sem, recv_sem=recv_sem,
            device_id=(mz, mx, my, other), device_id_type=MESH,
        ).wait_recv()

    def assembled(i, core):
        columns = [
            whole[i, core, :, g].astype(jnp.float32).reshape(PROBES, COLS) for g in range(NY)
        ]
        return jnp.concatenate(columns, axis=1).astype(jnp.bfloat16)

    def make_gain():
        loads[0].wait()
        for c in range(B // BLOCK):
            columns = pl.ds(c * BLOCK, BLOCK)
            below = pl.ds(c * BLOCK, B - c * BLOCK)
            for j in range(PIV - 1):
                gain[j, :, columns] = matmul(right[j, :, below], inverse[below, columns]).astype(jnp.bfloat16)

    def apply_future(i, p):
        for k, (dx, dy) in enumerate(PLANE):
            px, py = shifted(NX - dx, NY - dy)
            receive(whole.at[i, other, px, py], far_send_sem.at[i, k], far_recv_sem.at[i, k])
        receive(whole.at[i, other, mx, my], far_send_sem.at[i, len(PLANE)], far_recv_sem.at[i, len(PLANE)])
        both = jnp.concatenate([assembled(i, 0), assembled(i, 1)], axis=0)
        half = B // NC
        for f in range(2):
            weights = matmul_t(both[:, :half], future_left[0, f, p]) + matmul_t(
                both[:, half:], future_left[1, f, p]
            )
            weights = jnp.where(future_rank_ids < future_ranks_ref[f, p], weights, 0.0)
            future[f] = future[f] - matmul(weights.astype(jnp.bfloat16), future_right[f, p])

    outs = []
    for i, p in enumerate(reversed(range(PIV))):
        is_root = owner_ref[p] == me
        masked = jnp.where(is_root, acc[...], 0.0).reshape(NX, GROUP, B).astype(jnp.bfloat16)
        for g in range(NY):
            rs_send[i, :, g] = masked[:, :, g * COLS : (g + 1) * COLS]
        for k, (dx, dy) in enumerate(PLANE):
            px, py = shifted(dx, dy)
            send(
                rs_send.at[i, px, py], rs_recv.at[i, k],
                rs_send_sem.at[i, k], rs_recv_sem.at[i, k], (mz, px, py, mc),
            )
        if i == 0:
            swap.start()
            make_gain()
            loads[1].wait()
        else:
            if i == 1:
                swap_in.wait_recv()
                for load in loads[2:]:
                    load.wait()
            apply_future(i - 1, p + 1)

        part = rs_send[i, mx, my].astype(jnp.float32)
        for k in range(len(PLANE)):
            receive(rs_recv.at[i, k], rs_send_sem.at[i, k], rs_recv_sem.at[i, k])
            part = part + rs_recv[i, k].astype(jnp.float32)
        z_send[i] = part.astype(jnp.bfloat16)
        for k, dz in enumerate(COLUMN):
            send(
                z_send.at[i], z_recv.at[i, k], z_send_sem.at[i, k], z_recv_sem.at[i, k],
                (lax.rem(mz + dz, NZ), mx, my, mc),
            )
        for k in range(len(COLUMN)):
            receive(z_recv.at[i, k], z_send_sem.at[i, k], z_recv_sem.at[i, k])
            part = part + z_recv[i, k].astype(jnp.float32)
        whole[i, mc, mx, my] = part.astype(jnp.bfloat16)
        piece = whole.at[i, mc, mx, my]
        for k, (dx, dy) in enumerate(PLANE):
            px, py = shifted(dx, dy)
            send(piece, piece, own_send_sem.at[i, k], own_recv_sem.at[i, k], (mz, px, py, mc))
        for k, (dx, dy) in enumerate(PLANE):
            px, py = shifted(dx, dy)
            send(piece, piece, far_send_sem.at[i, k], far_recv_sem.at[i, k], (mz, px, py, other))
        last = len(PLANE)
        send(piece, piece, far_send_sem.at[i, last], far_recv_sem.at[i, last], (mz, mx, my, other))
        for k, (dx, dy) in enumerate(PLANE):
            px, py = shifted(NX - dx, NY - dy)
            receive(whole.at[i, mc, px, py], own_send_sem.at[i, k], own_recv_sem.at[i, k])
        columns = assembled(i, mc)
        block[i] = columns
        out = pltpu.make_async_copy(block.at[i], solved_ref.at[p], out_sem.at[i])
        out.start()
        outs.append(out)
        if p > 0:
            entry = jnp.clip(p - own_pivot - 1, 0, PIV - 2)
            active = holds * (own_pivot < p).astype(jnp.int32)
            factor = matmul_t(columns, left[entry])
            factor = jnp.where(rank_ids < coupling_ranks_ref[0, entry] * active, factor, 0.0)
            acc[...] = acc[...] - matmul(factor.astype(jnp.bfloat16), gain[entry])
    apply_future(PIV - 1, 0)
    out = pltpu.make_async_copy(future, future_out_ref, out_sem.at[PIV])
    out.start()
    outs.append(out)
    for copy in sent:
        copy.wait_send()
    swap.wait_send()
    for out in outs:
        out.wait()


def local(
    pivot_rhs, pivot_inverse, pivot_owner, coupling_left, coupling_right, coupling_ranks,
    future_left, future_right, future_ranks, future_rhs,
):
    smem = pl.BlockSpec(memory_space=pltpu.SMEM)
    hbm = pl.BlockSpec(memory_space=pl.ANY)
    plane, column = len(PLANE), len(COLUMN)
    dma = pltpu.SemaphoreType.DMA
    bf16, f32 = jnp.bfloat16, jnp.float32
    solved, future_out = pl.pallas_call(
        kernel,
        out_shape=(
            jax.ShapeDtypeStruct((PIV, PROBES, B), bf16),
            jax.ShapeDtypeStruct(future_rhs.shape, f32),
        ),
        in_specs=[smem] * 3 + [hbm] * 7,
        out_specs=(hbm, hbm),
        scratch_shapes=[
            pltpu.VMEM((B, B), bf16),
            pltpu.VMEM((PROBES, B), f32),
            pltpu.VMEM((PIV - 1, R, B), bf16),
            pltpu.VMEM((PIV - 1, R, B), bf16),
            pltpu.VMEM((NC, *future_left.shape), bf16),
            pltpu.VMEM(future_right.shape, bf16),
            pltpu.VMEM(future_rhs.shape, f32),
            pltpu.VMEM((PIV - 1, R, B), bf16),
            pltpu.VMEM((PROBES, B), f32),
            pltpu.VMEM((PIV, PROBES, B), bf16),
            pltpu.VMEM((PIV, NX, NY, GROUP, COLS), bf16),
            pltpu.VMEM((PIV, plane, GROUP, COLS), bf16),
            pltpu.VMEM((PIV, GROUP, COLS), bf16),
            pltpu.VMEM((PIV, column, GROUP, COLS), bf16),
            pltpu.VMEM((PIV, NC, NX, NY, GROUP, COLS), bf16),
            dma((6,)),
            dma((B // BLOCK,)),
            dma((PIV + 1,)),
            dma((2,)),
            dma((PIV, plane)),
            dma((PIV, plane)),
            dma((PIV, column)),
            dma((PIV, column)),
            dma((PIV, plane)),
            dma((PIV, plane)),
            dma((PIV, plane + 1)),
            dma((PIV, plane + 1)),
        ],
        compiler_params=pltpu.CompilerParams(collective_id=0, has_side_effects=True),
    )(
        pivot_owner,
        coupling_ranks,
        future_ranks,
        pivot_rhs[0].T,
        pivot_inverse[0],
        coupling_left[0].swapaxes(1, 2),
        coupling_right[0].swapaxes(1, 2),
        future_left,
        future_right,
        future_rhs,
    )
    return solved.swapaxes(1, 2), future_out


def solution(mesh):
    finer = Mesh(mesh.devices.reshape(NZ, NX, NY, NC), (*TC, "pr"))
    in_specs = (
        P(TC, None, "pr"),
        P(TC, None, None),
        P(),
        P(TC, None, None, None),
        P(TC, None, None, None),
        P(TC, None),
        P(TC, None, None, "pr"),
        P(TC, None, None, "pr"),
        P(TC, None),
        P(TC, None, "pr"),
    )
    out_specs = (P(None, None, "pr"), P(TC, None, "pr"))
    return jax.shard_map(local, mesh=finer, in_specs=in_specs, out_specs=out_specs, check_vma=False)
```

```python
import functools

import jax
import jax.numpy as jnp
from jax import lax
from jax.experimental import pallas as pl
from jax.experimental.pallas import tpu as pltpu
from jax.sharding import Mesh
from jax.sharding import PartitionSpec as P

TC = ("tz", "tx", "ty")
MESH = pl.DeviceIdType.MESH
NZ, NX, NY, NC = 8, 4, 4, 2
PIV, B, PROBES, R = 3, 1536, 32, 200
GROUP, COLS = PROBES // NX, B // NY
RANKS = 56
BLOCK = 256


def ring_distance(step, size):
    return min(step, size - step)


PLANE = sorted(
    ((dx, dy) for dx in range(NX) for dy in range(NY) if (dx, dy) != (0, 0)),
    key=lambda d: -(ring_distance(d[0], NX) + ring_distance(d[1], NY)),
)
COLUMN = sorted(range(1, NZ), key=lambda d: -ring_distance(d, NZ))
RING = (2, 1, 3)


def matmul(a, b):
    return lax.dot_general(a, b, (((1,), (0,)), ((), ())), preferred_element_type=jnp.float32)


def matmul_t(a, b):
    return lax.dot_general(a, b, (((1,), (1,)), ((), ())), preferred_element_type=jnp.float32)


def kernel(
    owner_ref, coupling_ranks_ref, future_ranks_ref,
    rhs_ref, inverse_ref, left_ref, right_ref, future_left_ref, future_right_ref, future_rhs_ref,
    solved_ref, future_out_ref,
    inverse, rhs, left, right, future_left, future_right, future, gain, acc, block,
    rs_send, rs_recv, z_send, z_recv, whole,
    pair_send, pair_recv, pair, rest_send, rest_recv, f_send, f_recv,
    load_sem, panel_sem, out_sem, swap_sem,
    rs_send_sem, rs_recv_sem, z_send_sem, z_recv_sem,
    own_send_sem, own_recv_sem, far_send_sem, far_recv_sem,
    pair_send_sem, pair_recv_sem, near_send_sem, near_recv_sem, cross_send_sem, cross_recv_sem,
    rest_send_sem, rest_recv_sem, f_send_sem, f_recv_sem,
):
    mz, mx, my, mc = (lax.axis_index(name) for name in (*TC, "pr"))
    me = (mz * NX + mx) * NY + my
    other = 1 - mc

    def shifted(dx, dy):
        return lax.rem(mx + dx, NX), lax.rem(my + dy, NY)

    rhs_load = pltpu.make_async_copy(rhs_ref, rhs, load_sem.at[0])
    rhs_load.start()
    panels = []
    for k in range(B // BLOCK):
        rows, columns = pl.ds(k * BLOCK, BLOCK), pl.ds(0, (k + 1) * BLOCK)
        panel = pltpu.make_async_copy(
            inverse_ref.at[rows, columns], inverse.at[rows, columns], panel_sem.at[k]
        )
        panel.start()
        panels.append(panel)

    barrier = pltpu.get_barrier_semaphore()
    greeted = 0
    for dx, dy in PLANE:
        px, py = shifted(dx, dy)
        for core in (mc, other):
            pl.semaphore_signal(barrier, 1, device_id=(mz, px, py, core), device_id_type=MESH)
            greeted += 1
    for dz in COLUMN:
        pz = lax.rem(mz + dz, NZ)
        pl.semaphore_signal(barrier, 1, device_id=(pz, mx, my, mc), device_id_type=MESH)
        greeted += 1
    pl.semaphore_signal(barrier, 1, device_id=(mz, mx, my, other), device_id_type=MESH)
    greeted += 1

    loads = [
        pltpu.make_async_copy(right_ref, right, load_sem.at[1]),
        pltpu.make_async_copy(left_ref, left, load_sem.at[2]),
        pltpu.make_async_copy(future_left_ref, future_left.at[mc], load_sem.at[3]),
        pltpu.make_async_copy(future_right_ref, future_right, load_sem.at[4]),
        pltpu.make_async_copy(future_rhs_ref, future, load_sem.at[5]),
    ]

    for load in loads[:2]:
        load.start()
    rhs_load.wait()
    start = rhs[...].astype(jnp.bfloat16)
    sums = [None] * (B // BLOCK)
    for k in range(B // BLOCK):
        panels[k].wait()
        piece = start[:, k * BLOCK : (k + 1) * BLOCK]
        for c in range(k + 1):
            term = matmul(piece, inverse[k * BLOCK : (k + 1) * BLOCK, c * BLOCK : (c + 1) * BLOCK])
            sums[c] = term if sums[c] is None else sums[c] + term
    for c in range(B // BLOCK):
        acc[:, c * BLOCK : (c + 1) * BLOCK] = sums[c]
    for load in loads[2:]:
        load.start()
    pl.semaphore_wait(barrier, greeted)

    swap = pltpu.make_async_remote_copy(
        src_ref=future_left_ref,
        dst_ref=future_left.at[mc],
        send_sem=swap_sem.at[0],
        recv_sem=swap_sem.at[1],
        device_id=(mz, mx, my, other),
        device_id_type=MESH,
    )
    swap_in = pltpu.make_async_remote_copy(
        src_ref=future_left_ref,
        dst_ref=future_left.at[other],
        send_sem=swap_sem.at[0],
        recv_sem=swap_sem.at[1],
        device_id=(mz, mx, my, other),
        device_id_type=MESH,
    )

    own_pivot = jnp.int32(0)
    holds = jnp.int32(0)
    for p in range(PIV):
        mine = (owner_ref[p] == me).astype(jnp.int32)
        own_pivot = own_pivot + mine * p
        holds = holds + mine
    rank_ids = lax.broadcasted_iota(jnp.int32, (PROBES, R), 1)
    future_rank_ids = lax.broadcasted_iota(jnp.int32, (NC * PROBES, R), 1)

    sent = []

    def send(src, dst, send_sem, recv_sem, device):
        copy = pltpu.make_async_remote_copy(
            src_ref=src, dst_ref=dst, send_sem=send_sem, recv_sem=recv_sem,
            device_id=device, device_id_type=MESH,
        )
        copy.start()
        sent.append(copy)

    def receive(dst, send_sem, recv_sem):
        pltpu.make_async_remote_copy(
            src_ref=dst, dst_ref=dst, send_sem=send_sem, recv_sem=recv_sem,
            device_id=(mz, mx, my, other), device_id_type=MESH,
        ).wait_recv()

    def assembled(i, core):
        columns = [
            whole[i, core, :, g].astype(jnp.float32).reshape(PROBES, COLS) for g in range(NY)
        ]
        return jnp.concatenate(columns, axis=1).astype(jnp.bfloat16)

    def make_gain(j):
        for c in range(B // BLOCK):
            columns = pl.ds(c * BLOCK, BLOCK)
            below = pl.ds(c * BLOCK, B - c * BLOCK)
            gain[j, :, columns] = matmul(right[j, :, below], inverse[below, columns]).astype(jnp.bfloat16)

    def spread_pair():
        limit = jnp.where(owner_ref[0] == me, coupling_ranks_ref[0, 0], 0)
        for x in range(NX):
            count = min(RANKS, R - x * RANKS)
            rows = pl.ds(x * RANKS, count)
            ids = lax.broadcasted_iota(jnp.int32, (count, COLS), 0) + x * RANKS
            for y in range(NY):
                columns = pl.ds(y * COLS, COLS)
                value = jnp.where(
                    mc == 0, left[0, rows, columns].astype(jnp.float32), gain[0, rows, columns].astype(jnp.float32)
                )
                pair_send[x, y, pl.ds(0, count)] = jnp.where(ids < limit, value, 0.0).astype(jnp.bfloat16)
                if count < RANKS:
                    pair_send[x, y, pl.ds(count, RANKS - count)] = jnp.zeros((RANKS - count, COLS), jnp.bfloat16)
        for k, (dx, dy) in enumerate(PLANE):
            px, py = shifted(dx, dy)
            send(
                pair_send.at[px, py], pair_recv.at[k], pair_send_sem.at[k], pair_recv_sem.at[k],
                (mz, px, py, mc),
            )

    def share_pair():
        total = pair_send[mx, my].astype(jnp.float32)
        for k in range(len(PLANE)):
            receive(pair_recv.at[k], pair_send_sem.at[k], pair_recv_sem.at[k])
            total = total + pair_recv[k].astype(jnp.float32)
        pair[mc, mx] = total.astype(jnp.bfloat16)
        piece = pair.at[mc, mx]
        for k, d in enumerate(RING):
            px = lax.rem(mx + d, NX)
            send(piece, piece, near_send_sem.at[k], near_recv_sem.at[k], (mz, px, my, mc))
            send(piece, piece, cross_send_sem.at[k], cross_recv_sem.at[k], (mz, px, my, other))
        last = len(RING)
        send(piece, piece, cross_send_sem.at[last], cross_recv_sem.at[last], (mz, mx, my, other))

    def take_pair():
        for k, d in enumerate(RING):
            px = lax.rem(mx + NX - d, NX)
            receive(pair.at[mc, px], near_send_sem.at[k], near_recv_sem.at[k])
            receive(pair.at[other, px], cross_send_sem.at[k], cross_recv_sem.at[k])
        last = len(RING)
        receive(pair.at[other, mx], cross_send_sem.at[last], cross_recv_sem.at[last])

    def apply_future(i, p):
        for k, (dx, dy) in enumerate(PLANE):
            px, py = shifted(NX - dx, NY - dy)
            receive(whole.at[i, other, px, py], far_send_sem.at[i, k], far_recv_sem.at[i, k])
        receive(whole.at[i, other, mx, my], far_send_sem.at[i, len(PLANE)], far_recv_sem.at[i, len(PLANE)])
        both = jnp.concatenate([assembled(i, 0), assembled(i, 1)], axis=0)
        half = B // NC
        for f in range(2):
            weights = matmul_t(both[:, :half], future_left[0, f, p]) + matmul_t(
                both[:, half:], future_left[1, f, p]
            )
            weights = jnp.where(future_rank_ids < future_ranks_ref[f, p], weights, 0.0)
            future[f] = future[f] - matmul(weights.astype(jnp.bfloat16), future_right[f, p])

    def scatter(i, p):
        masked = jnp.where(owner_ref[p] == me, acc[...], 0.0).reshape(NX, GROUP, B).astype(jnp.bfloat16)
        for g in range(NY):
            rs_send[i, :, g] = masked[:, :, g * COLS : (g + 1) * COLS]
        for k, (dx, dy) in enumerate(PLANE):
            px, py = shifted(dx, dy)
            send(
                rs_send.at[i, px, py], rs_recv.at[i, k],
                rs_send_sem.at[i, k], rs_recv_sem.at[i, k], (mz, px, py, mc),
            )

    def scattered(i):
        part = rs_send[i, mx, my].astype(jnp.float32)
        for k in range(len(PLANE)):
            receive(rs_recv.at[i, k], rs_send_sem.at[i, k], rs_recv_sem.at[i, k])
            part = part + rs_recv[i, k].astype(jnp.float32)
        return part

    def send_column(i, part):
        z_send[i] = part.astype(jnp.bfloat16)
        for k, dz in enumerate(COLUMN):
            send(
                z_send.at[i], z_recv.at[i, k], z_send_sem.at[i, k], z_recv_sem.at[i, k],
                (lax.rem(mz + dz, NZ), mx, my, mc),
            )

    def column_sum(i, part):
        for k in range(len(COLUMN)):
            receive(z_recv.at[i, k], z_send_sem.at[i, k], z_recv_sem.at[i, k])
            part = part + z_recv[i, k].astype(jnp.float32)
        part = part.astype(jnp.bfloat16)
        whole[i, mc, mx, my] = part
        return part

    def gather(i):
        piece = whole.at[i, mc, mx, my]
        for k, (dx, dy) in enumerate(PLANE):
            px, py = shifted(dx, dy)
            send(piece, piece, own_send_sem.at[i, k], own_recv_sem.at[i, k], (mz, px, py, mc))
        for k, (dx, dy) in enumerate(PLANE):
            px, py = shifted(dx, dy)
            send(piece, piece, far_send_sem.at[i, k], far_recv_sem.at[i, k], (mz, px, py, other))
        last = len(PLANE)
        send(piece, piece, far_send_sem.at[i, last], far_recv_sem.at[i, last], (mz, mx, my, other))

    outs = []

    def gathered(i, p):
        for k, (dx, dy) in enumerate(PLANE):
            px, py = shifted(NX - dx, NY - dy)
            receive(whole.at[i, mc, px, py], own_send_sem.at[i, k], own_recv_sem.at[i, k])
        columns = assembled(i, mc)
        block[i] = columns
        out = pltpu.make_async_copy(block.at[i], solved_ref.at[p], out_sem.at[i])
        out.start()
        outs.append(out)
        return columns

    scatter(0, 2)
    loads[0].wait()
    loads[1].wait()
    make_gain(0)
    spread_pair()
    swap.start()
    part = scattered(0)
    send_column(0, part)
    make_gain(1)
    column_sum(0, part)
    gather(0)
    columns = gathered(0, 2)
    entry = jnp.clip(2 - own_pivot - 1, 0, PIV - 2)
    active = holds * (own_pivot < 2).astype(jnp.int32)
    factor = matmul_t(columns, left[entry])
    factor = jnp.where(rank_ids < coupling_ranks_ref[0, entry] * active, factor, 0.0)
    acc[...] = acc[...] - matmul(factor.astype(jnp.bfloat16), gain[entry])

    scatter(1, 1)
    rest = jnp.where(owner_ref[0] == me, acc[...], 0.0).reshape(NX, GROUP, B)
    for g in range(NY):
        rest_send[:, g] = rest[:, :, g * COLS : (g + 1) * COLS]
    for k, (dx, dy) in enumerate(PLANE):
        px, py = shifted(dx, dy)
        send(
            rest_send.at[px, py], rest_recv.at[k], rest_send_sem.at[k], rest_recv_sem.at[k],
            (mz, px, py, mc),
        )
    share_pair()
    part = scattered(1)
    send_column(1, part)
    swap_in.wait_recv()
    for load in loads[2:]:
        load.wait()
    apply_future(0, 2)
    slice_1 = column_sum(1, part)

    take_pair()
    for x in range(NX):
        f_send[x] = matmul_t(slice_1, pair[0, x])
    for k, d in enumerate(RING):
        send(
            f_send, f_recv.at[k], f_send_sem.at[k], f_recv_sem.at[k],
            (mz, mx, lax.rem(my + d, NY), mc),
        )
    gather(1)
    part = rest_send[mx, my]
    for k in range(len(PLANE)):
        receive(rest_recv.at[k], rest_send_sem.at[k], rest_recv_sem.at[k])
        part = part + rest_recv[k]
    for k in range(len(RING)):
        receive(f_recv.at[k], f_send_sem.at[k], f_recv_sem.at[k])
    for x in range(NX):
        factor = f_send[x]
        for k in range(len(RING)):
            factor = factor + f_recv[k, x]
        part = part - matmul(factor.astype(jnp.bfloat16), pair[1, x])
    send_column(2, part)
    gathered(1, 1)
    apply_future(1, 1)
    column_sum(2, part)
    gather(2)
    gathered(2, 0)
    apply_future(PIV - 1, 0)
    out = pltpu.make_async_copy(future, future_out_ref, out_sem.at[PIV])
    out.start()
    outs.append(out)
    for copy in sent:
        copy.wait_send()
    swap.wait_send()
    for out in outs:
        out.wait()


def local(
    pivot_rhs, pivot_inverse, pivot_owner, coupling_left, coupling_right, coupling_ranks,
    future_left, future_right, future_ranks, future_rhs,
):
    smem = pl.BlockSpec(memory_space=pltpu.SMEM)
    hbm = pl.BlockSpec(memory_space=pl.ANY)
    plane, column, ring = len(PLANE), len(COLUMN), len(RING)
    dma = pltpu.SemaphoreType.DMA
    bf16, f32 = jnp.bfloat16, jnp.float32
    solved, future_out = pl.pallas_call(
        kernel,
        out_shape=(
            jax.ShapeDtypeStruct((PIV, PROBES, B), bf16),
            jax.ShapeDtypeStruct(future_rhs.shape, f32),
        ),
        in_specs=[smem] * 3 + [hbm] * 7,
        out_specs=(hbm, hbm),
        scratch_shapes=[
            pltpu.VMEM((B, B), bf16),
            pltpu.VMEM((PROBES, B), f32),
            pltpu.VMEM((PIV - 1, R, B), bf16),
            pltpu.VMEM((PIV - 1, R, B), bf16),
            pltpu.VMEM((NC, *future_left.shape), bf16),
            pltpu.VMEM(future_right.shape, bf16),
            pltpu.VMEM(future_rhs.shape, f32),
            pltpu.VMEM((PIV - 1, R, B), bf16),
            pltpu.VMEM((PROBES, B), f32),
            pltpu.VMEM((PIV, PROBES, B), bf16),
            pltpu.VMEM((PIV - 1, NX, NY, GROUP, COLS), bf16),
            pltpu.VMEM((PIV - 1, plane, GROUP, COLS), bf16),
            pltpu.VMEM((PIV, GROUP, COLS), bf16),
            pltpu.VMEM((PIV, column, GROUP, COLS), bf16),
            pltpu.VMEM((PIV, NC, NX, NY, GROUP, COLS), bf16),
            pltpu.VMEM((NX, NY, RANKS, COLS), bf16),
            pltpu.VMEM((plane, RANKS, COLS), bf16),
            pltpu.VMEM((NC, NX, RANKS, COLS), bf16),
            pltpu.VMEM((NX, NY, GROUP, COLS), f32),
            pltpu.VMEM((plane, GROUP, COLS), f32),
            pltpu.VMEM((NX, GROUP, RANKS), f32),
            pltpu.VMEM((ring, NX, GROUP, RANKS), f32),
            dma((6,)),
            dma((B // BLOCK,)),
            dma((PIV + 1,)),
            dma((2,)),
            dma((PIV - 1, plane)),
            dma((PIV - 1, plane)),
            dma((PIV, column)),
            dma((PIV, column)),
            dma((PIV, plane)),
            dma((PIV, plane)),
            dma((PIV, plane + 1)),
            dma((PIV, plane + 1)),
            dma((plane,)),
            dma((plane,)),
            dma((ring,)),
            dma((ring,)),
            dma((ring + 1,)),
            dma((ring + 1,)),
            dma((plane,)),
            dma((plane,)),
            dma((ring,)),
            dma((ring,)),
        ],
        compiler_params=pltpu.CompilerParams(collective_id=0, has_side_effects=True),
    )(
        pivot_owner,
        coupling_ranks,
        future_ranks,
        pivot_rhs[0].T,
        pivot_inverse[0],
        coupling_left[0].swapaxes(1, 2),
        coupling_right[0].swapaxes(1, 2),
        future_left,
        future_right,
        future_rhs,
    )
    return solved.swapaxes(1, 2), future_out


def solution(mesh):
    finer = Mesh(mesh.devices.reshape(NZ, NX, NY, NC), (*TC, "pr"))
    in_specs = (
        P(TC, None, "pr"),
        P(TC, None, None),
        P(),
        P(TC, None, None, None),
        P(TC, None, None, None),
        P(TC, None),
        P(TC, None, None, "pr"),
        P(TC, None, None, "pr"),
        P(TC, None),
        P(TC, None, "pr"),
    )
    out_specs = (P(None, None, "pr"), P(TC, None, "pr"))
    return jax.shard_map(local, mesh=finer, in_specs=in_specs, out_specs=out_specs, check_vma=False)
```

```python
import functools

import jax
import jax.numpy as jnp
from jax import lax
from jax.experimental import pallas as pl
from jax.experimental.pallas import tpu as pltpu
from jax.sharding import Mesh
from jax.sharding import PartitionSpec as P

TC = ("tz", "tx", "ty")
MESH = pl.DeviceIdType.MESH
NZ, NX, NY, NC = 8, 4, 4, 2
PIV, B, PROBES, R = 3, 1536, 32, 200
GROUP, COLS = PROBES // NX, B // NY
RANKS = 56
BLOCK = 256


def ring_distance(step, size):
    return min(step, size - step)


PLANE = sorted(
    ((dx, dy) for dx in range(NX) for dy in range(NY) if (dx, dy) != (0, 0)),
    key=lambda d: -(ring_distance(d[0], NX) + ring_distance(d[1], NY)),
)
COLUMN = sorted(range(1, NZ), key=lambda d: -ring_distance(d, NZ))
RING = (2, 1, 3)


def matmul(a, b):
    return lax.dot_general(a, b, (((1,), (0,)), ((), ())), preferred_element_type=jnp.float32)


def matmul_t(a, b):
    return lax.dot_general(a, b, (((1,), (1,)), ((), ())), preferred_element_type=jnp.float32)


def kernel(
    owner_ref, coupling_ranks_ref, future_ranks_ref,
    rhs_ref, inverse_ref, left_ref, right_ref, future_left_ref, future_right_ref, future_rhs_ref,
    solved_ref, future_out_ref,
    inverse, rhs, left, right, future_left, future_right, future, gain, acc, block,
    rs_send, rs_recv, z_send, z_recv, whole,
    pair_send, pair_recv, pair_mid, pair_last, pair, rest_send, rest_recv, f_send, f_recv,
    load_sem, panel_sem, out_sem, swap_sem,
    rs_send_sem, rs_recv_sem, z_send_sem, z_recv_sem,
    own_send_sem, own_recv_sem, far_send_sem, far_recv_sem,
    pair_send_sem, pair_recv_sem, mid_send_sem, mid_recv_sem, near_send_sem, near_recv_sem, cross_send_sem, cross_recv_sem,
    rest_send_sem, rest_recv_sem, f_send_sem, f_recv_sem,
):
    mz, mx, my, mc = (lax.axis_index(name) for name in (*TC, "pr"))
    me = (mz * NX + mx) * NY + my
    other = 1 - mc

    def shifted(dx, dy):
        return lax.rem(mx + dx, NX), lax.rem(my + dy, NY)

    rhs_load = pltpu.make_async_copy(rhs_ref, rhs, load_sem.at[0])
    rhs_load.start()
    panels = []
    for k in range(B // BLOCK):
        rows, columns = pl.ds(k * BLOCK, BLOCK), pl.ds(0, (k + 1) * BLOCK)
        panel = pltpu.make_async_copy(
            inverse_ref.at[rows, columns], inverse.at[rows, columns], panel_sem.at[k]
        )
        panel.start()
        panels.append(panel)

    barrier = pltpu.get_barrier_semaphore()
    greeted = 0
    for dx, dy in PLANE:
        px, py = shifted(dx, dy)
        for core in (mc, other):
            pl.semaphore_signal(barrier, 1, device_id=(mz, px, py, core), device_id_type=MESH)
            greeted += 1
    for dz in COLUMN:
        pz = lax.rem(mz + dz, NZ)
        pl.semaphore_signal(barrier, 1, device_id=(pz, mx, my, mc), device_id_type=MESH)
        greeted += 1
    pl.semaphore_signal(barrier, 1, device_id=(mz, mx, my, other), device_id_type=MESH)
    greeted += 1

    loads = [
        pltpu.make_async_copy(right_ref, right, load_sem.at[1]),
        pltpu.make_async_copy(left_ref, left, load_sem.at[2]),
        pltpu.make_async_copy(future_left_ref, future_left.at[mc], load_sem.at[3]),
        pltpu.make_async_copy(future_right_ref, future_right, load_sem.at[4]),
        pltpu.make_async_copy(future_rhs_ref, future, load_sem.at[5]),
    ]

    for load in loads[:2]:
        load.start()
    rhs_load.wait()
    start = rhs[...].astype(jnp.bfloat16)
    sums = [None] * (B // BLOCK)
    for k in range(B // BLOCK):
        panels[k].wait()
        piece = start[:, k * BLOCK : (k + 1) * BLOCK]
        for c in range(k + 1):
            term = matmul(piece, inverse[k * BLOCK : (k + 1) * BLOCK, c * BLOCK : (c + 1) * BLOCK])
            sums[c] = term if sums[c] is None else sums[c] + term
    for c in range(B // BLOCK):
        acc[:, c * BLOCK : (c + 1) * BLOCK] = sums[c]
    for load in loads[2:]:
        load.start()
    pl.semaphore_wait(barrier, greeted)

    swap = pltpu.make_async_remote_copy(
        src_ref=future_left_ref,
        dst_ref=future_left.at[mc],
        send_sem=swap_sem.at[0],
        recv_sem=swap_sem.at[1],
        device_id=(mz, mx, my, other),
        device_id_type=MESH,
    )
    swap_in = pltpu.make_async_remote_copy(
        src_ref=future_left_ref,
        dst_ref=future_left.at[other],
        send_sem=swap_sem.at[0],
        recv_sem=swap_sem.at[1],
        device_id=(mz, mx, my, other),
        device_id_type=MESH,
    )

    own_pivot = jnp.int32(0)
    holds = jnp.int32(0)
    for p in range(PIV):
        mine = (owner_ref[p] == me).astype(jnp.int32)
        own_pivot = own_pivot + mine * p
        holds = holds + mine
    rank_ids = lax.broadcasted_iota(jnp.int32, (PROBES, R), 1)
    future_rank_ids = lax.broadcasted_iota(jnp.int32, (NC * PROBES, R), 1)

    sent = []

    def send(src, dst, send_sem, recv_sem, device):
        copy = pltpu.make_async_remote_copy(
            src_ref=src, dst_ref=dst, send_sem=send_sem, recv_sem=recv_sem,
            device_id=device, device_id_type=MESH,
        )
        copy.start()
        sent.append(copy)

    def receive(dst, send_sem, recv_sem):
        pltpu.make_async_remote_copy(
            src_ref=dst, dst_ref=dst, send_sem=send_sem, recv_sem=recv_sem,
            device_id=(mz, mx, my, other), device_id_type=MESH,
        ).wait_recv()

    def assembled(i, core):
        columns = [
            whole[i, core, :, g].astype(jnp.float32).reshape(PROBES, COLS) for g in range(NY)
        ]
        return jnp.concatenate(columns, axis=1).astype(jnp.bfloat16)

    def make_gain(j):
        for c in range(B // BLOCK):
            columns = pl.ds(c * BLOCK, BLOCK)
            below = pl.ds(c * BLOCK, B - c * BLOCK)
            gain[j, :, columns] = matmul(right[j, :, below], inverse[below, columns]).astype(jnp.bfloat16)

    first, second = mx + mc * (my - mx), my + mc * (mx - my)

    def along_first(d):
        return mz, lax.rem(mx + d * other, NX), lax.rem(my + d * mc, NY), mc

    def along_second(d):
        return mz, lax.rem(mx + d * mc, NX), lax.rem(my + d * other, NY), mc

    def make_pair():
        limit = jnp.where(owner_ref[0] == me, coupling_ranks_ref[0, 0], 0)

        def factor_slice(ref, x, y, count):
            return ref[0, pl.ds(x * RANKS, count), pl.ds(y * COLS, COLS)].astype(jnp.float32)

        for a in range(NX):
            for b in range(NY):
                row, col = min(RANKS, R - a * RANKS), min(RANKS, R - b * RANKS)
                ids = lax.broadcasted_iota(jnp.int32, (RANKS, COLS), 0)
                left_part = factor_slice(left, a, b, row)
                right_part = factor_slice(gain, b, a, col)
                if row < RANKS:
                    left_part = jnp.concatenate([left_part, jnp.zeros((RANKS - row, COLS), jnp.float32)])
                if col < RANKS:
                    right_part = jnp.concatenate([right_part, jnp.zeros((RANKS - col, COLS), jnp.float32)])
                value = jnp.where(mc == 0, left_part, right_part)
                start = (a + mc * (b - a)) * RANKS
                pair_send[a, b] = jnp.where(ids + start < limit, value, 0.0).astype(jnp.bfloat16)

    def spread_pair():
        for k, d in enumerate(RING):
            to = lax.rem(first + d, NX)
            send(pair_send.at[to], pair_recv.at[k], pair_send_sem.at[k], pair_recv_sem.at[k], along_first(d))

    def spread_on():
        for k in range(len(RING)):
            receive(pair_recv.at[k], pair_send_sem.at[k], pair_recv_sem.at[k])
        total = pair_send[first].astype(jnp.float32)
        for k in range(len(RING)):
            total = total + pair_recv[k].astype(jnp.float32)
        pair_mid[...] = total.astype(jnp.bfloat16)
        for k, d in enumerate(RING):
            to = lax.rem(second + d, NY)
            send(pair_mid.at[to], pair_last.at[k], mid_send_sem.at[k], mid_recv_sem.at[k], along_second(d))

    def share_pair():
        total = pair_mid[second].astype(jnp.float32)
        for k in range(len(RING)):
            receive(pair_last.at[k], mid_send_sem.at[k], mid_recv_sem.at[k])
            total = total + pair_last[k].astype(jnp.float32)
        pair[mc, mx] = total.astype(jnp.bfloat16)
        piece = pair.at[mc, mx]
        for k, d in enumerate(RING):
            px = lax.rem(mx + d, NX)
            send(piece, piece, near_send_sem.at[k], near_recv_sem.at[k], (mz, px, my, mc))
            send(piece, piece, cross_send_sem.at[k], cross_recv_sem.at[k], (mz, px, my, other))
        last = len(RING)
        send(piece, piece, cross_send_sem.at[last], cross_recv_sem.at[last], (mz, mx, my, other))

    def take_pair():
        for k, d in enumerate(RING):
            px = lax.rem(mx + NX - d, NX)
            receive(pair.at[mc, px], near_send_sem.at[k], near_recv_sem.at[k])
            receive(pair.at[other, px], cross_send_sem.at[k], cross_recv_sem.at[k])
        last = len(RING)
        receive(pair.at[other, mx], cross_send_sem.at[last], cross_recv_sem.at[last])

    def apply_future(i, p):
        for k, (dx, dy) in enumerate(PLANE):
            px, py = shifted(NX - dx, NY - dy)
            receive(whole.at[i, other, px, py], far_send_sem.at[i, k], far_recv_sem.at[i, k])
        receive(whole.at[i, other, mx, my], far_send_sem.at[i, len(PLANE)], far_recv_sem.at[i, len(PLANE)])
        both = jnp.concatenate([assembled(i, 0), assembled(i, 1)], axis=0)
        half = B // NC
        for f in range(2):
            weights = matmul_t(both[:, :half], future_left[0, f, p]) + matmul_t(
                both[:, half:], future_left[1, f, p]
            )
            weights = jnp.where(future_rank_ids < future_ranks_ref[f, p], weights, 0.0)
            future[f] = future[f] - matmul(weights.astype(jnp.bfloat16), future_right[f, p])

    def scatter(i, p):
        masked = jnp.where(owner_ref[p] == me, acc[...], 0.0).reshape(NX, GROUP, B).astype(jnp.bfloat16)
        for g in range(NY):
            rs_send[i, :, g] = masked[:, :, g * COLS : (g + 1) * COLS]
        for k, (dx, dy) in enumerate(PLANE):
            px, py = shifted(dx, dy)
            send(
                rs_send.at[i, px, py], rs_recv.at[i, k],
                rs_send_sem.at[i, k], rs_recv_sem.at[i, k], (mz, px, py, mc),
            )

    def scattered(i):
        part = rs_send[i, mx, my].astype(jnp.float32)
        for k in range(len(PLANE)):
            receive(rs_recv.at[i, k], rs_send_sem.at[i, k], rs_recv_sem.at[i, k])
            part = part + rs_recv[i, k].astype(jnp.float32)
        return part

    def send_column(i, part):
        z_send[i] = part.astype(jnp.bfloat16)
        for k, dz in enumerate(COLUMN):
            send(
                z_send.at[i], z_recv.at[i, k], z_send_sem.at[i, k], z_recv_sem.at[i, k],
                (lax.rem(mz + dz, NZ), mx, my, mc),
            )

    def column_sum(i, part):
        for k in range(len(COLUMN)):
            receive(z_recv.at[i, k], z_send_sem.at[i, k], z_recv_sem.at[i, k])
            part = part + z_recv[i, k].astype(jnp.float32)
        part = part.astype(jnp.bfloat16)
        whole[i, mc, mx, my] = part
        return part

    def gather(i):
        piece = whole.at[i, mc, mx, my]
        for k, (dx, dy) in enumerate(PLANE):
            px, py = shifted(dx, dy)
            send(piece, piece, own_send_sem.at[i, k], own_recv_sem.at[i, k], (mz, px, py, mc))
    def gather_far(i):
        piece = whole.at[i, mc, mx, my]
        for k, (dx, dy) in enumerate(PLANE):
            px, py = shifted(dx, dy)
            send(piece, piece, far_send_sem.at[i, k], far_recv_sem.at[i, k], (mz, px, py, other))
        last = len(PLANE)
        send(piece, piece, far_send_sem.at[i, last], far_recv_sem.at[i, last], (mz, mx, my, other))

    outs = []

    def gathered(i, p):
        for k, (dx, dy) in enumerate(PLANE):
            px, py = shifted(NX - dx, NY - dy)
            receive(whole.at[i, mc, px, py], own_send_sem.at[i, k], own_recv_sem.at[i, k])
        columns = assembled(i, mc)
        block[i] = columns
        out = pltpu.make_async_copy(block.at[i], solved_ref.at[p], out_sem.at[i])
        out.start()
        outs.append(out)
        return columns

    scatter(0, 2)
    loads[0].wait()
    loads[1].wait()
    make_gain(0)
    make_pair()
    spread_pair()
    swap.start()
    part = scattered(0)
    send_column(0, part)
    make_gain(1)
    column_sum(0, part)
    gather(0)
    spread_on()
    columns = gathered(0, 2)
    entry = jnp.clip(2 - own_pivot - 1, 0, PIV - 2)
    active = holds * (own_pivot < 2).astype(jnp.int32)
    factor = matmul_t(columns, left[entry])
    factor = jnp.where(rank_ids < coupling_ranks_ref[0, entry] * active, factor, 0.0)
    acc[...] = acc[...] - matmul(factor.astype(jnp.bfloat16), gain[entry])

    scatter(1, 1)
    rest = jnp.where(owner_ref[0] == me, acc[...], 0.0).reshape(NX, GROUP, B)
    for g in range(NY):
        rest_send[:, g] = rest[:, :, g * COLS : (g + 1) * COLS]
    for k, (dx, dy) in enumerate(PLANE):
        px, py = shifted(dx, dy)
        send(
            rest_send.at[px, py], rest_recv.at[k], rest_send_sem.at[k], rest_recv_sem.at[k],
            (mz, px, py, mc),
        )
    share_pair()
    part = scattered(1)
    send_column(1, part)
    gather_far(0)
    swap_in.wait_recv()
    for load in loads[2:]:
        load.wait()
    slice_1 = column_sum(1, part)

    take_pair()
    for x in range(NX):
        f_send[x] = matmul_t(slice_1, pair[0, x])
    for k, d in enumerate(RING):
        send(
            f_send, f_recv.at[k], f_send_sem.at[k], f_recv_sem.at[k],
            (mz, mx, lax.rem(my + d, NY), mc),
        )
    gather(1)
    gather_far(1)
    part = rest_send[mx, my]
    for k in range(len(PLANE)):
        receive(rest_recv.at[k], rest_send_sem.at[k], rest_recv_sem.at[k])
        part = part + rest_recv[k]
    for k in range(len(RING)):
        receive(f_recv.at[k], f_send_sem.at[k], f_recv_sem.at[k])
    for x in range(NX):
        factor = f_send[x]
        for k in range(len(RING)):
            factor = factor + f_recv[k, x]
        part = part - matmul(factor.astype(jnp.bfloat16), pair[1, x])
    send_column(2, part)
    gathered(1, 1)
    apply_future(0, 2)
    apply_future(1, 1)
    column_sum(2, part)
    gather(2)
    gather_far(2)
    gathered(2, 0)
    apply_future(PIV - 1, 0)
    out = pltpu.make_async_copy(future, future_out_ref, out_sem.at[PIV])
    out.start()
    outs.append(out)
    for copy in sent:
        copy.wait_send()
    swap.wait_send()
    for out in outs:
        out.wait()


def local(
    pivot_rhs, pivot_inverse, pivot_owner, coupling_left, coupling_right, coupling_ranks,
    future_left, future_right, future_ranks, future_rhs,
):
    smem = pl.BlockSpec(memory_space=pltpu.SMEM)
    hbm = pl.BlockSpec(memory_space=pl.ANY)
    plane, column, ring = len(PLANE), len(COLUMN), len(RING)
    dma = pltpu.SemaphoreType.DMA
    bf16, f32 = jnp.bfloat16, jnp.float32
    solved, future_out = pl.pallas_call(
        kernel,
        out_shape=(
            jax.ShapeDtypeStruct((PIV, PROBES, B), bf16),
            jax.ShapeDtypeStruct(future_rhs.shape, f32),
        ),
        in_specs=[smem] * 3 + [hbm] * 7,
        out_specs=(hbm, hbm),
        scratch_shapes=[
            pltpu.VMEM((B, B), bf16),
            pltpu.VMEM((PROBES, B), f32),
            pltpu.VMEM((PIV - 1, R, B), bf16),
            pltpu.VMEM((PIV - 1, R, B), bf16),
            pltpu.VMEM((NC, *future_left.shape), bf16),
            pltpu.VMEM(future_right.shape, bf16),
            pltpu.VMEM(future_rhs.shape, f32),
            pltpu.VMEM((PIV - 1, R, B), bf16),
            pltpu.VMEM((PROBES, B), f32),
            pltpu.VMEM((PIV, PROBES, B), bf16),
            pltpu.VMEM((PIV - 1, NX, NY, GROUP, COLS), bf16),
            pltpu.VMEM((PIV - 1, plane, GROUP, COLS), bf16),
            pltpu.VMEM((PIV, GROUP, COLS), bf16),
            pltpu.VMEM((PIV, column, GROUP, COLS), bf16),
            pltpu.VMEM((PIV, NC, NX, NY, GROUP, COLS), bf16),
            pltpu.VMEM((NX, NY, RANKS, COLS), bf16),
            pltpu.VMEM((ring, NY, RANKS, COLS), bf16),
            pltpu.VMEM((NY, RANKS, COLS), bf16),
            pltpu.VMEM((ring, RANKS, COLS), bf16),
            pltpu.VMEM((NC, NX, RANKS, COLS), bf16),
            pltpu.VMEM((NX, NY, GROUP, COLS), f32),
            pltpu.VMEM((plane, GROUP, COLS), f32),
            pltpu.VMEM((NX, GROUP, RANKS), f32),
            pltpu.VMEM((ring, NX, GROUP, RANKS), f32),
            dma((6,)),
            dma((B // BLOCK,)),
            dma((PIV + 1,)),
            dma((2,)),
            dma((PIV - 1, plane)),
            dma((PIV - 1, plane)),
            dma((PIV, column)),
            dma((PIV, column)),
            dma((PIV, plane)),
            dma((PIV, plane)),
            dma((PIV, plane + 1)),
            dma((PIV, plane + 1)),
            dma((ring,)),
            dma((ring,)),
            dma((ring,)),
            dma((ring,)),
            dma((ring,)),
            dma((ring,)),
            dma((ring + 1,)),
            dma((ring + 1,)),
            dma((plane,)),
            dma((plane,)),
            dma((ring,)),
            dma((ring,)),
        ],
        compiler_params=pltpu.CompilerParams(collective_id=0, has_side_effects=True),
    )(
        pivot_owner,
        coupling_ranks,
        future_ranks,
        pivot_rhs[0].T,
        pivot_inverse[0],
        coupling_left[0].swapaxes(1, 2),
        coupling_right[0].swapaxes(1, 2),
        future_left,
        future_right,
        future_rhs,
    )
    return solved.swapaxes(1, 2), future_out


def solution(mesh):
    finer = Mesh(mesh.devices.reshape(NZ, NX, NY, NC), (*TC, "pr"))
    in_specs = (
        P(TC, None, "pr"),
        P(TC, None, None),
        P(),
        P(TC, None, None, None),
        P(TC, None, None, None),
        P(TC, None),
        P(TC, None, None, "pr"),
        P(TC, None, None, "pr"),
        P(TC, None),
        P(TC, None, "pr"),
    )
    out_specs = (P(None, None, "pr"), P(TC, None, "pr"))
    return jax.shard_map(local, mesh=finer, in_specs=in_specs, out_specs=out_specs, check_vma=False)
```

```python
import functools

import jax
import jax.numpy as jnp
from jax import lax
from jax.experimental import pallas as pl
from jax.experimental.pallas import tpu as pltpu
from jax.sharding import Mesh
from jax.sharding import PartitionSpec as P

TC = ("tz", "tx", "ty")
MESH = pl.DeviceIdType.MESH
NZ, NX, NY, NC = 8, 4, 4, 2
PIV, B, PROBES, R = 3, 1536, 32, 200
GROUP, COLS = PROBES // NX, B // NY
RANKS = 56
BLOCK = 256


def ring_distance(step, size):
    return min(step, size - step)


PLANE = sorted(
    ((dx, dy) for dx in range(NX) for dy in range(NY) if (dx, dy) != (0, 0)),
    key=lambda d: -(ring_distance(d[0], NX) + ring_distance(d[1], NY)),
)
COLUMN = sorted(range(1, NZ), key=lambda d: -ring_distance(d, NZ))
RING = (2, 1, 3)


def matmul(a, b):
    return lax.dot_general(a, b, (((1,), (0,)), ((), ())), preferred_element_type=jnp.float32)


def matmul_t(a, b):
    return lax.dot_general(a, b, (((1,), (1,)), ((), ())), preferred_element_type=jnp.float32)


def kernel(
    owner_ref, coupling_ranks_ref, future_ranks_ref,
    rhs_ref, inverse_ref, left_ref, right_ref, future_left_ref, future_right_ref, future_rhs_ref,
    solved_ref, future_out_ref,
    inverse, rhs, left, right, future_left, future_right, future, gain, acc, block,
    rs_send, rs_recv, z_send, z_recv, whole,
    pair_send, pair_recv, pair_mid, pair_last, pair, rest_send, rest_recv, f_send, f_recv,
    load_sem, panel_sem, out_sem, swap_sem,
    rs_send_sem, rs_recv_sem, z_send_sem, z_recv_sem,
    own_send_sem, own_recv_sem, far_send_sem, far_recv_sem,
    pair_send_sem, pair_recv_sem, mid_send_sem, mid_recv_sem, near_send_sem, near_recv_sem, cross_send_sem, cross_recv_sem,
    rest_send_sem, rest_recv_sem, f_send_sem, f_recv_sem,
):
    mz, mx, my, mc = (lax.axis_index(name) for name in (*TC, "pr"))
    me = (mz * NX + mx) * NY + my
    other = 1 - mc

    def shifted(dx, dy):
        return lax.rem(mx + dx, NX), lax.rem(my + dy, NY)

    rhs_load = pltpu.make_async_copy(rhs_ref, rhs, load_sem.at[0])
    rhs_load.start()
    panels = []
    for k in range(B // BLOCK):
        rows, columns = pl.ds(k * BLOCK, BLOCK), pl.ds(0, (k + 1) * BLOCK)
        panel = pltpu.make_async_copy(
            inverse_ref.at[rows, columns], inverse.at[rows, columns], panel_sem.at[k]
        )
        panel.start()
        panels.append(panel)

    barrier = pltpu.get_barrier_semaphore()
    greeted = 0
    for dx, dy in PLANE:
        px, py = shifted(dx, dy)
        for core in (mc, other):
            pl.semaphore_signal(barrier, 1, device_id=(mz, px, py, core), device_id_type=MESH)
            greeted += 1
    for dz in COLUMN:
        pz = lax.rem(mz + dz, NZ)
        pl.semaphore_signal(barrier, 1, device_id=(pz, mx, my, mc), device_id_type=MESH)
        greeted += 1
    pl.semaphore_signal(barrier, 1, device_id=(mz, mx, my, other), device_id_type=MESH)
    greeted += 1

    loads = [
        pltpu.make_async_copy(right_ref, right, load_sem.at[1]),
        pltpu.make_async_copy(left_ref, left, load_sem.at[2]),
        pltpu.make_async_copy(future_left_ref, future_left.at[mc], load_sem.at[3]),
        pltpu.make_async_copy(future_right_ref, future_right, load_sem.at[4]),
        pltpu.make_async_copy(future_rhs_ref, future, load_sem.at[5]),
    ]

    for load in loads[:2]:
        load.start()
    rhs_load.wait()
    start = rhs[...].astype(jnp.bfloat16)
    sums = [None] * (B // BLOCK)
    for k in range(B // BLOCK):
        panels[k].wait()
        piece = start[:, k * BLOCK : (k + 1) * BLOCK]
        for c in range(k + 1):
            term = matmul(piece, inverse[k * BLOCK : (k + 1) * BLOCK, c * BLOCK : (c + 1) * BLOCK])
            sums[c] = term if sums[c] is None else sums[c] + term
    for c in range(B // BLOCK):
        acc[:, c * BLOCK : (c + 1) * BLOCK] = sums[c]
    for load in loads[2:]:
        load.start()
    pl.semaphore_wait(barrier, greeted)

    swap = pltpu.make_async_remote_copy(
        src_ref=future_left_ref,
        dst_ref=future_left.at[mc],
        send_sem=swap_sem.at[0],
        recv_sem=swap_sem.at[1],
        device_id=(mz, mx, my, other),
        device_id_type=MESH,
    )
    swap_in = pltpu.make_async_remote_copy(
        src_ref=future_left_ref,
        dst_ref=future_left.at[other],
        send_sem=swap_sem.at[0],
        recv_sem=swap_sem.at[1],
        device_id=(mz, mx, my, other),
        device_id_type=MESH,
    )

    own_pivot = jnp.int32(0)
    holds = jnp.int32(0)
    for p in range(PIV):
        mine = (owner_ref[p] == me).astype(jnp.int32)
        own_pivot = own_pivot + mine * p
        holds = holds + mine
    rank_ids = lax.broadcasted_iota(jnp.int32, (PROBES, R), 1)
    future_rank_ids = lax.broadcasted_iota(jnp.int32, (NC * PROBES, R), 1)

    sent = []

    def send(src, dst, send_sem, recv_sem, device):
        copy = pltpu.make_async_remote_copy(
            src_ref=src, dst_ref=dst, send_sem=send_sem, recv_sem=recv_sem,
            device_id=device, device_id_type=MESH,
        )
        copy.start()
        sent.append(copy)

    def receive(dst, send_sem, recv_sem):
        pltpu.make_async_remote_copy(
            src_ref=dst, dst_ref=dst, send_sem=send_sem, recv_sem=recv_sem,
            device_id=(mz, mx, my, other), device_id_type=MESH,
        ).wait_recv()

    def assembled(i, core):
        columns = [
            whole[i, core, :, g].astype(jnp.float32).reshape(PROBES, COLS) for g in range(NY)
        ]
        return jnp.concatenate(columns, axis=1).astype(jnp.bfloat16)

    def make_gain(j):
        for c in range(B // BLOCK):
            columns = pl.ds(c * BLOCK, BLOCK)
            below = pl.ds(c * BLOCK, B - c * BLOCK)
            gain[j, :, columns] = matmul(right[j, :, below], inverse[below, columns]).astype(jnp.bfloat16)

    first, second = mx + mc * (my - mx), my + mc * (mx - my)

    def along_first(d):
        return mz, lax.rem(mx + d * other, NX), lax.rem(my + d * mc, NY), mc

    def along_second(d):
        return mz, lax.rem(mx + d * mc, NX), lax.rem(my + d * other, NY), mc

    def make_pair():
        limit = jnp.where(owner_ref[0] == me, coupling_ranks_ref[0, 0], 0)

        def factor_slice(ref, x, y, count):
            return ref[0, pl.ds(x * RANKS, count), pl.ds(y * COLS, COLS)].astype(jnp.float32)

        for a in range(NX):
            for b in range(NY):
                row, col = min(RANKS, R - a * RANKS), min(RANKS, R - b * RANKS)
                ids = lax.broadcasted_iota(jnp.int32, (RANKS, COLS), 0)
                left_part = factor_slice(left, a, b, row)
                right_part = factor_slice(gain, b, a, col)
                if row < RANKS:
                    left_part = jnp.concatenate([left_part, jnp.zeros((RANKS - row, COLS), jnp.float32)])
                if col < RANKS:
                    right_part = jnp.concatenate([right_part, jnp.zeros((RANKS - col, COLS), jnp.float32)])
                value = jnp.where(mc == 0, left_part, right_part)
                start = (a + mc * (b - a)) * RANKS
                pair_send[a, b] = jnp.where(ids + start < limit, value, 0.0).astype(jnp.bfloat16)

    def spread_pair():
        for k, d in enumerate(RING):
            to = lax.rem(first + d, NX)
            send(pair_send.at[to], pair_recv.at[k], pair_send_sem.at[k], pair_recv_sem.at[k], along_first(d))

    def spread_on():
        for k in range(len(RING)):
            receive(pair_recv.at[k], pair_send_sem.at[k], pair_recv_sem.at[k])
        total = pair_send[first].astype(jnp.float32)
        for k in range(len(RING)):
            total = total + pair_recv[k].astype(jnp.float32)
        pair_mid[...] = total.astype(jnp.bfloat16)
        for k, d in enumerate(RING):
            to = lax.rem(second + d, NY)
            send(pair_mid.at[to], pair_last.at[k], mid_send_sem.at[k], mid_recv_sem.at[k], along_second(d))

    def share_pair():
        total = pair_mid[second].astype(jnp.float32)
        for k in range(len(RING)):
            receive(pair_last.at[k], mid_send_sem.at[k], mid_recv_sem.at[k])
            total = total + pair_last[k].astype(jnp.float32)
        pair[mc, mx] = total.astype(jnp.bfloat16)
        piece = pair.at[mc, mx]
        for k, d in enumerate(RING):
            px = lax.rem(mx + d, NX)
            send(piece, piece, near_send_sem.at[k], near_recv_sem.at[k], (mz, px, my, mc))
            send(piece, piece, cross_send_sem.at[k], cross_recv_sem.at[k], (mz, px, my, other))
        last = len(RING)
        send(piece, piece, cross_send_sem.at[last], cross_recv_sem.at[last], (mz, mx, my, other))

    def take_pair():
        for k, d in enumerate(RING):
            px = lax.rem(mx + NX - d, NX)
            receive(pair.at[mc, px], near_send_sem.at[k], near_recv_sem.at[k])
            receive(pair.at[other, px], cross_send_sem.at[k], cross_recv_sem.at[k])
        last = len(RING)
        receive(pair.at[other, mx], cross_send_sem.at[last], cross_recv_sem.at[last])

    def take_far(i):
        for k, (dx, dy) in enumerate(PLANE):
            px, py = shifted(NX - dx, NY - dy)
            receive(whole.at[i, other, px, py], far_send_sem.at[i, k], far_recv_sem.at[i, k])
        receive(whole.at[i, other, mx, my], far_send_sem.at[i, len(PLANE)], far_recv_sem.at[i, len(PLANE)])

    half = B // NC

    def weighted(probes, f, p, ids):
        weights = matmul_t(probes[:, :half], future_left[0, f, p]) + matmul_t(
            probes[:, half:], future_left[1, f, p]
        )
        weights = jnp.where(ids < future_ranks_ref[f, p], weights, 0.0)
        return matmul(weights.astype(jnp.bfloat16), future_right[f, p])

    def apply_future(i, p):
        take_far(i)
        both = jnp.concatenate([assembled(i, 0), assembled(i, 1)], axis=0)
        for f in range(2):
            future[f] = future[f] - weighted(both, f, p, future_rank_ids)

    def apply_future_half(p, core, probes, f):
        rows = pl.ds(pl.multiple_of(core * PROBES, PROBES), PROBES)
        future[f, rows] = future[f, rows] - weighted(probes, f, p, rank_ids)

    def scatter(i, p):
        masked = jnp.where(owner_ref[p] == me, acc[...], 0.0).reshape(NX, GROUP, B).astype(jnp.bfloat16)
        for g in range(NY):
            rs_send[i, :, g] = masked[:, :, g * COLS : (g + 1) * COLS]
        for k, (dx, dy) in enumerate(PLANE):
            px, py = shifted(dx, dy)
            send(
                rs_send.at[i, px, py], rs_recv.at[i, k],
                rs_send_sem.at[i, k], rs_recv_sem.at[i, k], (mz, px, py, mc),
            )

    def scattered(i):
        part = rs_send[i, mx, my].astype(jnp.float32)
        for k in range(len(PLANE)):
            receive(rs_recv.at[i, k], rs_send_sem.at[i, k], rs_recv_sem.at[i, k])
            part = part + rs_recv[i, k].astype(jnp.float32)
        return part

    def send_column(i, part):
        z_send[i] = part.astype(jnp.bfloat16)
        for k, dz in enumerate(COLUMN):
            send(
                z_send.at[i], z_recv.at[i, k], z_send_sem.at[i, k], z_recv_sem.at[i, k],
                (lax.rem(mz + dz, NZ), mx, my, mc),
            )

    def column_sum(i, part):
        for k in range(len(COLUMN)):
            receive(z_recv.at[i, k], z_send_sem.at[i, k], z_recv_sem.at[i, k])
            part = part + z_recv[i, k].astype(jnp.float32)
        part = part.astype(jnp.bfloat16)
        whole[i, mc, mx, my] = part
        return part

    def gather(i):
        piece = whole.at[i, mc, mx, my]
        for k, (dx, dy) in enumerate(PLANE):
            px, py = shifted(dx, dy)
            send(piece, piece, own_send_sem.at[i, k], own_recv_sem.at[i, k], (mz, px, py, mc))
    def gather_far(i):
        piece = whole.at[i, mc, mx, my]
        for k, (dx, dy) in enumerate(PLANE):
            px, py = shifted(dx, dy)
            send(piece, piece, far_send_sem.at[i, k], far_recv_sem.at[i, k], (mz, px, py, other))
        last = len(PLANE)
        send(piece, piece, far_send_sem.at[i, last], far_recv_sem.at[i, last], (mz, mx, my, other))

    outs = []

    def gathered(i, p):
        for k, (dx, dy) in enumerate(PLANE):
            px, py = shifted(NX - dx, NY - dy)
            receive(whole.at[i, mc, px, py], own_send_sem.at[i, k], own_recv_sem.at[i, k])
        columns = assembled(i, mc)
        block[i] = columns
        out = pltpu.make_async_copy(block.at[i], solved_ref.at[p], out_sem.at[i])
        out.start()
        outs.append(out)
        return columns

    scatter(0, 2)
    loads[0].wait()
    loads[1].wait()
    make_gain(0)
    make_pair()
    spread_pair()
    swap.start()
    part = scattered(0)
    send_column(0, part)
    make_gain(1)
    column_sum(0, part)
    gather(0)
    spread_on()
    columns = gathered(0, 2)
    entry = jnp.clip(2 - own_pivot - 1, 0, PIV - 2)
    active = holds * (own_pivot < 2).astype(jnp.int32)
    factor = matmul_t(columns, left[entry])
    factor = jnp.where(rank_ids < coupling_ranks_ref[0, entry] * active, factor, 0.0)
    acc[...] = acc[...] - matmul(factor.astype(jnp.bfloat16), gain[entry])

    scatter(1, 1)
    rest = jnp.where(owner_ref[0] == me, acc[...], 0.0).reshape(NX, GROUP, B)
    for g in range(NY):
        rest_send[:, g] = rest[:, :, g * COLS : (g + 1) * COLS]
    for k, (dx, dy) in enumerate(PLANE):
        px, py = shifted(dx, dy)
        send(
            rest_send.at[px, py], rest_recv.at[k], rest_send_sem.at[k], rest_recv_sem.at[k],
            (mz, px, py, mc),
        )
    share_pair()
    part = scattered(1)
    send_column(1, part)
    gather_far(0)
    swap_in.wait_recv()
    for load in loads[2:]:
        load.wait()
    slice_1 = column_sum(1, part)

    take_pair()
    for x in range(NX):
        f_send[x] = matmul_t(slice_1, pair[0, x])
    for k, d in enumerate(RING):
        send(
            f_send, f_recv.at[k], f_send_sem.at[k], f_recv_sem.at[k],
            (mz, mx, lax.rem(my + d, NY), mc),
        )
    gather(1)
    gather_far(1)
    part = rest_send[mx, my]
    for k in range(len(PLANE)):
        receive(rest_recv.at[k], rest_send_sem.at[k], rest_recv_sem.at[k])
        part = part + rest_recv[k]
    for k in range(len(RING)):
        receive(f_recv.at[k], f_send_sem.at[k], f_recv_sem.at[k])
    for x in range(NX):
        factor = f_send[x]
        for k in range(len(RING)):
            factor = factor + f_recv[k, x]
        part = part - matmul(factor.astype(jnp.bfloat16), pair[1, x])
    send_column(2, part)
    gathered(1, 1)
    apply_future(0, 2)
    apply_future(1, 1)
    column_sum(2, part)
    gather(2)
    gather_far(2)
    columns = gathered(2, 0)

    def store(f):
        out = pltpu.make_async_copy(future.at[f], future_out_ref.at[f], out_sem.at[PIV + f])
        out.start()
        outs.append(out)

    for f in range(2):
        apply_future_half(0, mc, columns, f)
    take_far(PIV - 1)
    columns = assembled(PIV - 1, other)
    for f in range(2):
        apply_future_half(0, other, columns, f)
        store(f)
    for copy in sent:
        copy.wait_send()
    swap.wait_send()
    for out in outs:
        out.wait()


def deliver(solved_ref, future_ref, solved_out_ref, future_out_ref, solved, future, in_sem, out_sem):
    pairs = [(solved_ref.at[p], solved.at[p], solved_out_ref.at[p]) for p in range(PIV)]
    pairs += [(future_ref.at[f], future.at[f], future_out_ref.at[f]) for f in range(2)]
    arrivals = [pltpu.make_async_copy(a, b, in_sem.at[k]) for k, (a, b, _) in enumerate(pairs)]
    leavings = [pltpu.make_async_copy(b, c, out_sem.at[k]) for k, (_, b, c) in enumerate(pairs)]
    for arrival in arrivals:
        arrival.start()
    for arrival, leaving in zip(arrivals, leavings, strict=True):
        arrival.wait()
        leaving.start()
    for leaving in leavings:
        leaving.wait()


def local(
    pivot_rhs, pivot_inverse, pivot_owner, coupling_left, coupling_right, coupling_ranks,
    future_left, future_right, future_ranks, future_rhs,
):
    smem = pl.BlockSpec(memory_space=pltpu.SMEM)
    hbm = pl.BlockSpec(memory_space=pl.ANY)
    plane, column, ring = len(PLANE), len(COLUMN), len(RING)
    dma = pltpu.SemaphoreType.DMA
    bf16, f32 = jnp.bfloat16, jnp.float32
    solved, future_out = pl.pallas_call(
        kernel,
        out_shape=(
            jax.ShapeDtypeStruct((PIV, PROBES, B), bf16),
            jax.ShapeDtypeStruct(future_rhs.shape, f32),
        ),
        in_specs=[smem] * 3 + [hbm] * 7,
        out_specs=(hbm, hbm),
        scratch_shapes=[
            pltpu.VMEM((B, B), bf16),
            pltpu.VMEM((PROBES, B), f32),
            pltpu.VMEM((PIV - 1, R, B), bf16),
            pltpu.VMEM((PIV - 1, R, B), bf16),
            pltpu.VMEM((NC, *future_left.shape), bf16),
            pltpu.VMEM(future_right.shape, bf16),
            pltpu.VMEM(future_rhs.shape, f32),
            pltpu.VMEM((PIV - 1, R, B), bf16),
            pltpu.VMEM((PROBES, B), f32),
            pltpu.VMEM((PIV, PROBES, B), bf16),
            pltpu.VMEM((PIV - 1, NX, NY, GROUP, COLS), bf16),
            pltpu.VMEM((PIV - 1, plane, GROUP, COLS), bf16),
            pltpu.VMEM((PIV, GROUP, COLS), bf16),
            pltpu.VMEM((PIV, column, GROUP, COLS), bf16),
            pltpu.VMEM((PIV, NC, NX, NY, GROUP, COLS), bf16),
            pltpu.VMEM((NX, NY, RANKS, COLS), bf16),
            pltpu.VMEM((ring, NY, RANKS, COLS), bf16),
            pltpu.VMEM((NY, RANKS, COLS), bf16),
            pltpu.VMEM((ring, RANKS, COLS), bf16),
            pltpu.VMEM((NC, NX, RANKS, COLS), bf16),
            pltpu.VMEM((NX, NY, GROUP, COLS), f32),
            pltpu.VMEM((plane, GROUP, COLS), f32),
            pltpu.VMEM((NX, GROUP, RANKS), f32),
            pltpu.VMEM((ring, NX, GROUP, RANKS), f32),
            dma((6,)),
            dma((B // BLOCK,)),
            dma((PIV + 2,)),
            dma((2,)),
            dma((PIV - 1, plane)),
            dma((PIV - 1, plane)),
            dma((PIV, column)),
            dma((PIV, column)),
            dma((PIV, plane)),
            dma((PIV, plane)),
            dma((PIV, plane + 1)),
            dma((PIV, plane + 1)),
            dma((ring,)),
            dma((ring,)),
            dma((ring,)),
            dma((ring,)),
            dma((ring,)),
            dma((ring,)),
            dma((ring + 1,)),
            dma((ring + 1,)),
            dma((plane,)),
            dma((plane,)),
            dma((ring,)),
            dma((ring,)),
        ],
        compiler_params=pltpu.CompilerParams(collective_id=0, has_side_effects=True),
    )(
        pivot_owner,
        coupling_ranks,
        future_ranks,
        pivot_rhs[0].T,
        pivot_inverse[0],
        coupling_left[0].swapaxes(1, 2),
        coupling_right[0].swapaxes(1, 2),
        future_left,
        future_right,
        future_rhs,
    )
    solved, future_out = pl.pallas_call(
        deliver,
        out_shape=(
            jax.ShapeDtypeStruct(solved.shape, bf16),
            jax.ShapeDtypeStruct(future_out.shape, f32),
        ),
        in_specs=[hbm, hbm],
        out_specs=(hbm, hbm),
        scratch_shapes=[
            pltpu.VMEM(solved.shape, bf16),
            pltpu.VMEM(future_out.shape, f32),
            dma((PIV + 2,)),
            dma((PIV + 2,)),
        ],
    )(solved, future_out)
    return solved.swapaxes(1, 2), future_out


def solution(mesh):
    finer = Mesh(mesh.devices.reshape(NZ, NX, NY, NC), (*TC, "pr"))
    in_specs = (
        P(TC, None, "pr"),
        P(TC, None, None),
        P(),
        P(TC, None, None, None),
        P(TC, None, None, None),
        P(TC, None),
        P(TC, None, None, "pr"),
        P(TC, None, None, "pr"),
        P(TC, None),
        P(TC, None, "pr"),
    )
    out_specs = (P(None, None, "pr"), P(TC, None, "pr"))
    return jax.shard_map(local, mesh=finer, in_specs=in_specs, out_specs=out_specs, check_vma=False)
```

```python
import functools

import jax
import jax.numpy as jnp
from jax import lax
from jax.experimental import pallas as pl
from jax.experimental.pallas import tpu as pltpu
from jax.sharding import Mesh
from jax.sharding import PartitionSpec as P

TC = ("tz", "tx", "ty")
MESH = pl.DeviceIdType.MESH
NZ, NX, NY, NC = 8, 4, 4, 2
PIV, B, PROBES, R = 3, 1536, 32, 200
GROUP, COLS = PROBES // NX, B // NY
RANKS = 56
BLOCK = 256


def ring_distance(step, size):
    return min(step, size - step)


PLANE = sorted(
    ((dx, dy) for dx in range(NX) for dy in range(NY) if (dx, dy) != (0, 0)),
    key=lambda d: -(ring_distance(d[0], NX) + ring_distance(d[1], NY)),
)
COLUMN = sorted(range(1, NZ), key=lambda d: -ring_distance(d, NZ))
RING = (2, 1, 3)


def matmul(a, b):
    return lax.dot_general(a, b, (((1,), (0,)), ((), ())), preferred_element_type=jnp.float32)


def matmul_t(a, b):
    return lax.dot_general(a, b, (((1,), (1,)), ((), ())), preferred_element_type=jnp.float32)


def kernel(
    owner_in, coupling_ranks_in, future_ranks_in,
    rhs_ref, inverse_ref, left_ref, right_ref, future_left_ref, future_right_ref, future_rhs_ref,
    solved_ref, future_out_ref,
    inverse, rhs, left, right, future_left, future_right, future, gain, acc, block,
    rs_send, rs_recv, z_send, z_recv, whole,
    pair_send, pair_recv, pair_mid, pair_last, pair, rest_send, rest_recv, f_send, f_recv,
    owner_ref, coupling_ranks_ref, future_ranks_ref, table_sem,
    load_sem, panel_sem, out_sem, swap_sem,
    rs_send_sem, rs_recv_sem, z_send_sem, z_recv_sem,
    own_send_sem, own_recv_sem, far_send_sem, far_recv_sem,
    pair_send_sem, pair_recv_sem, mid_send_sem, mid_recv_sem, near_send_sem, near_recv_sem, cross_send_sem, cross_recv_sem,
    rest_send_sem, rest_recv_sem, f_send_sem, f_recv_sem,
):
    mz, mx, my, mc = (lax.axis_index(name) for name in (*TC, "pr"))
    me = (mz * NX + mx) * NY + my
    other = 1 - mc

    def shifted(dx, dy):
        return lax.rem(mx + dx, NX), lax.rem(my + dy, NY)

    barrier = pltpu.get_barrier_semaphore()
    greeted = 0
    for dx, dy in PLANE:
        px, py = shifted(dx, dy)
        for core in (mc, other):
            pl.semaphore_signal(barrier, 1, device_id=(mz, px, py, core), device_id_type=MESH)
            greeted += 1
    for dz in COLUMN:
        pz = lax.rem(mz + dz, NZ)
        pl.semaphore_signal(barrier, 1, device_id=(pz, mx, my, mc), device_id_type=MESH)
        greeted += 1
    pl.semaphore_signal(barrier, 1, device_id=(mz, mx, my, other), device_id_type=MESH)
    greeted += 1

    rhs_load = pltpu.make_async_copy(rhs_ref, rhs, load_sem.at[0])
    rhs_load.start()
    panels = []
    for k in range(B // BLOCK):
        rows, columns = pl.ds(k * BLOCK, BLOCK), pl.ds(0, (k + 1) * BLOCK)
        panel = pltpu.make_async_copy(
            inverse_ref.at[rows, columns], inverse.at[rows, columns], panel_sem.at[k]
        )
        panel.start()
        panels.append(panel)

    tables = [
        pltpu.make_async_copy(owner_in, owner_ref, table_sem.at[0]),
        pltpu.make_async_copy(coupling_ranks_in, coupling_ranks_ref, table_sem.at[1]),
        pltpu.make_async_copy(future_ranks_in, future_ranks_ref, table_sem.at[2]),
    ]
    for table in tables:
        table.start()

    loads = [
        pltpu.make_async_copy(right_ref, right, load_sem.at[1]),
        pltpu.make_async_copy(left_ref, left, load_sem.at[2]),
        pltpu.make_async_copy(future_left_ref, future_left.at[mc], load_sem.at[3]),
        pltpu.make_async_copy(future_right_ref, future_right, load_sem.at[4]),
        pltpu.make_async_copy(future_rhs_ref, future, load_sem.at[5]),
    ]

    for load in loads[:2]:
        load.start()
    rhs_load.wait()
    start = rhs[...].astype(jnp.bfloat16)
    sums = [None] * (B // BLOCK)
    for k in range(B // BLOCK):
        panels[k].wait()
        piece = start[:, k * BLOCK : (k + 1) * BLOCK]
        for c in range(k + 1):
            term = matmul(piece, inverse[k * BLOCK : (k + 1) * BLOCK, c * BLOCK : (c + 1) * BLOCK])
            sums[c] = term if sums[c] is None else sums[c] + term
    for c in range(B // BLOCK):
        acc[:, c * BLOCK : (c + 1) * BLOCK] = sums[c]
    for load in loads[2:]:
        load.start()
    pl.semaphore_wait(barrier, greeted)

    swap = pltpu.make_async_remote_copy(
        src_ref=future_left_ref,
        dst_ref=future_left.at[mc],
        send_sem=swap_sem.at[0],
        recv_sem=swap_sem.at[1],
        device_id=(mz, mx, my, other),
        device_id_type=MESH,
    )
    swap_in = pltpu.make_async_remote_copy(
        src_ref=future_left_ref,
        dst_ref=future_left.at[other],
        send_sem=swap_sem.at[0],
        recv_sem=swap_sem.at[1],
        device_id=(mz, mx, my, other),
        device_id_type=MESH,
    )

    for table in tables:
        table.wait()
    own_pivot = jnp.int32(0)
    holds = jnp.int32(0)
    for p in range(PIV):
        mine = (owner_ref[p] == me).astype(jnp.int32)
        own_pivot = own_pivot + mine * p
        holds = holds + mine
    rank_ids = lax.broadcasted_iota(jnp.int32, (PROBES, R), 1)
    future_rank_ids = lax.broadcasted_iota(jnp.int32, (NC * PROBES, R), 1)

    sent = []

    def send(src, dst, send_sem, recv_sem, device):
        copy = pltpu.make_async_remote_copy(
            src_ref=src, dst_ref=dst, send_sem=send_sem, recv_sem=recv_sem,
            device_id=device, device_id_type=MESH,
        )
        copy.start()
        sent.append(copy)

    def receive(dst, send_sem, recv_sem):
        pltpu.make_async_remote_copy(
            src_ref=dst, dst_ref=dst, send_sem=send_sem, recv_sem=recv_sem,
            device_id=(mz, mx, my, other), device_id_type=MESH,
        ).wait_recv()

    def assembled(i, core):
        columns = [
            whole[i, core, :, g].astype(jnp.float32).reshape(PROBES, COLS) for g in range(NY)
        ]
        return jnp.concatenate(columns, axis=1).astype(jnp.bfloat16)

    def make_gain(j):
        for c in range(B // BLOCK):
            columns = pl.ds(c * BLOCK, BLOCK)
            below = pl.ds(c * BLOCK, B - c * BLOCK)
            gain[j, :, columns] = matmul(right[j, :, below], inverse[below, columns]).astype(jnp.bfloat16)

    first, second = mx + mc * (my - mx), my + mc * (mx - my)

    def along_first(d):
        return mz, lax.rem(mx + d * other, NX), lax.rem(my + d * mc, NY), mc

    def along_second(d):
        return mz, lax.rem(mx + d * mc, NX), lax.rem(my + d * other, NY), mc

    def make_pair():
        limit = jnp.where(owner_ref[0] == me, coupling_ranks_ref[0, 0], 0)

        def factor_slice(ref, x, y, count):
            return ref[0, pl.ds(x * RANKS, count), pl.ds(y * COLS, COLS)].astype(jnp.float32)

        for a in range(NX):
            for b in range(NY):
                row, col = min(RANKS, R - a * RANKS), min(RANKS, R - b * RANKS)
                ids = lax.broadcasted_iota(jnp.int32, (RANKS, COLS), 0)
                left_part = factor_slice(left, a, b, row)
                right_part = factor_slice(gain, b, a, col)
                if row < RANKS:
                    left_part = jnp.concatenate([left_part, jnp.zeros((RANKS - row, COLS), jnp.float32)])
                if col < RANKS:
                    right_part = jnp.concatenate([right_part, jnp.zeros((RANKS - col, COLS), jnp.float32)])
                value = jnp.where(mc == 0, left_part, right_part)
                start = (a + mc * (b - a)) * RANKS
                pair_send[a, b] = jnp.where(ids + start < limit, value, 0.0).astype(jnp.bfloat16)

    def spread_pair():
        for k, d in enumerate(RING):
            to = lax.rem(first + d, NX)
            send(pair_send.at[to], pair_recv.at[k], pair_send_sem.at[k], pair_recv_sem.at[k], along_first(d))

    def spread_on():
        for k in range(len(RING)):
            receive(pair_recv.at[k], pair_send_sem.at[k], pair_recv_sem.at[k])
        total = pair_send[first].astype(jnp.float32)
        for k in range(len(RING)):
            total = total + pair_recv[k].astype(jnp.float32)
        pair_mid[...] = total.astype(jnp.bfloat16)
        for k, d in enumerate(RING):
            to = lax.rem(second + d, NY)
            send(pair_mid.at[to], pair_last.at[k], mid_send_sem.at[k], mid_recv_sem.at[k], along_second(d))

    def share_pair():
        total = pair_mid[second].astype(jnp.float32)
        for k in range(len(RING)):
            receive(pair_last.at[k], mid_send_sem.at[k], mid_recv_sem.at[k])
            total = total + pair_last[k].astype(jnp.float32)
        pair[mc, mx] = total.astype(jnp.bfloat16)
        piece = pair.at[mc, mx]
        for k, d in enumerate(RING):
            px = lax.rem(mx + d, NX)
            send(piece, piece, near_send_sem.at[k], near_recv_sem.at[k], (mz, px, my, mc))
            send(piece, piece, cross_send_sem.at[k], cross_recv_sem.at[k], (mz, px, my, other))
        last = len(RING)
        send(piece, piece, cross_send_sem.at[last], cross_recv_sem.at[last], (mz, mx, my, other))

    def take_pair():
        for k, d in enumerate(RING):
            px = lax.rem(mx + NX - d, NX)
            receive(pair.at[mc, px], near_send_sem.at[k], near_recv_sem.at[k])
            receive(pair.at[other, px], cross_send_sem.at[k], cross_recv_sem.at[k])
        last = len(RING)
        receive(pair.at[other, mx], cross_send_sem.at[last], cross_recv_sem.at[last])

    def take_far(i):
        for k, (dx, dy) in enumerate(PLANE):
            px, py = shifted(NX - dx, NY - dy)
            receive(whole.at[i, other, px, py], far_send_sem.at[i, k], far_recv_sem.at[i, k])
        receive(whole.at[i, other, mx, my], far_send_sem.at[i, len(PLANE)], far_recv_sem.at[i, len(PLANE)])

    half = B // NC

    def weighted(probes, f, p, ids):
        weights = matmul_t(probes[:, :half], future_left[0, f, p]) + matmul_t(
            probes[:, half:], future_left[1, f, p]
        )
        weights = jnp.where(ids < future_ranks_ref[f, p], weights, 0.0)
        return matmul(weights.astype(jnp.bfloat16), future_right[f, p])

    def apply_future(i, p):
        take_far(i)
        both = jnp.concatenate([assembled(i, 0), assembled(i, 1)], axis=0)
        for f in range(2):
            future[f] = future[f] - weighted(both, f, p, future_rank_ids)

    def apply_future_half(p, core, probes, f):
        rows = pl.ds(pl.multiple_of(core * PROBES, PROBES), PROBES)
        future[f, rows] = future[f, rows] - weighted(probes, f, p, rank_ids)

    def scatter(i, p):
        masked = jnp.where(owner_ref[p] == me, acc[...], 0.0).reshape(NX, GROUP, B).astype(jnp.bfloat16)
        for g in range(NY):
            rs_send[i, :, g] = masked[:, :, g * COLS : (g + 1) * COLS]
        for k, (dx, dy) in enumerate(PLANE):
            px, py = shifted(dx, dy)
            send(
                rs_send.at[i, px, py], rs_recv.at[i, k],
                rs_send_sem.at[i, k], rs_recv_sem.at[i, k], (mz, px, py, mc),
            )

    def scattered(i):
        part = rs_send[i, mx, my].astype(jnp.float32)
        for k in range(len(PLANE)):
            receive(rs_recv.at[i, k], rs_send_sem.at[i, k], rs_recv_sem.at[i, k])
            part = part + rs_recv[i, k].astype(jnp.float32)
        return part

    def send_column(i, part):
        z_send[i] = part.astype(jnp.bfloat16)
        for k, dz in enumerate(COLUMN):
            send(
                z_send.at[i], z_recv.at[i, k], z_send_sem.at[i, k], z_recv_sem.at[i, k],
                (lax.rem(mz + dz, NZ), mx, my, mc),
            )

    def column_sum(i, part):
        for k in range(len(COLUMN)):
            receive(z_recv.at[i, k], z_send_sem.at[i, k], z_recv_sem.at[i, k])
            part = part + z_recv[i, k].astype(jnp.float32)
        part = part.astype(jnp.bfloat16)
        whole[i, mc, mx, my] = part
        return part

    def gather(i):
        piece = whole.at[i, mc, mx, my]
        for k, (dx, dy) in enumerate(PLANE):
            px, py = shifted(dx, dy)
            send(piece, piece, own_send_sem.at[i, k], own_recv_sem.at[i, k], (mz, px, py, mc))
    def gather_far(i):
        piece = whole.at[i, mc, mx, my]
        for k, (dx, dy) in enumerate(PLANE):
            px, py = shifted(dx, dy)
            send(piece, piece, far_send_sem.at[i, k], far_recv_sem.at[i, k], (mz, px, py, other))
        last = len(PLANE)
        send(piece, piece, far_send_sem.at[i, last], far_recv_sem.at[i, last], (mz, mx, my, other))

    def gather_both(i):
        piece = whole.at[i, mc, mx, my]
        for k, (dx, dy) in enumerate(PLANE):
            px, py = shifted(dx, dy)
            send(piece, piece, own_send_sem.at[i, k], own_recv_sem.at[i, k], (mz, px, py, mc))
            send(piece, piece, far_send_sem.at[i, k], far_recv_sem.at[i, k], (mz, px, py, other))
        last = len(PLANE)
        send(piece, piece, far_send_sem.at[i, last], far_recv_sem.at[i, last], (mz, mx, my, other))

    outs = []

    def gathered(i, p):
        for k, (dx, dy) in enumerate(PLANE):
            px, py = shifted(NX - dx, NY - dy)
            receive(whole.at[i, mc, px, py], own_send_sem.at[i, k], own_recv_sem.at[i, k])
        columns = assembled(i, mc)
        block[i] = columns
        out = pltpu.make_async_copy(block.at[i], solved_ref.at[p], out_sem.at[i])
        out.start()
        outs.append(out)
        return columns

    scatter(0, 2)
    loads[0].wait()
    loads[1].wait()
    make_gain(0)
    make_pair()
    spread_pair()
    swap.start()
    part = scattered(0)
    send_column(0, part)
    make_gain(1)
    column_sum(0, part)
    gather(0)
    spread_on()
    columns = gathered(0, 2)
    entry = jnp.clip(2 - own_pivot - 1, 0, PIV - 2)
    active = holds * (own_pivot < 2).astype(jnp.int32)
    factor = matmul_t(columns, left[entry])
    factor = jnp.where(rank_ids < coupling_ranks_ref[0, entry] * active, factor, 0.0)
    acc[...] = acc[...] - matmul(factor.astype(jnp.bfloat16), gain[entry])

    scatter(1, 1)
    rest = jnp.where(owner_ref[0] == me, acc[...], 0.0).reshape(NX, GROUP, B)
    for g in range(NY):
        rest_send[:, g] = rest[:, :, g * COLS : (g + 1) * COLS]
    for k, (dx, dy) in enumerate(PLANE):
        px, py = shifted(dx, dy)
        send(
            rest_send.at[px, py], rest_recv.at[k], rest_send_sem.at[k], rest_recv_sem.at[k],
            (mz, px, py, mc),
        )
    share_pair()
    part = scattered(1)
    send_column(1, part)
    gather_far(0)
    swap_in.wait_recv()
    for load in loads[2:]:
        load.wait()
    slice_1 = column_sum(1, part)

    take_pair()
    for x in range(NX):
        f_send[x] = matmul_t(slice_1, pair[0, x])
    for k, d in enumerate(RING):
        send(
            f_send, f_recv.at[k], f_send_sem.at[k], f_recv_sem.at[k],
            (mz, mx, lax.rem(my + d, NY), mc),
        )
    gather(1)
    gather_far(1)
    part = rest_send[mx, my]
    for k in range(len(PLANE)):
        receive(rest_recv.at[k], rest_send_sem.at[k], rest_recv_sem.at[k])
        part = part + rest_recv[k]
    for k in range(len(RING)):
        receive(f_recv.at[k], f_send_sem.at[k], f_recv_sem.at[k])
    for x in range(NX):
        factor = f_send[x]
        for k in range(len(RING)):
            factor = factor + f_recv[k, x]
        part = part - matmul(factor.astype(jnp.bfloat16), pair[1, x])
    send_column(2, part)
    gathered(1, 1)
    apply_future(0, 2)
    apply_future(1, 1)
    column_sum(2, part)
    gather_both(2)
    columns = gathered(2, 0)

    def store(f):
        out = pltpu.make_async_copy(future.at[f], future_out_ref.at[f], out_sem.at[PIV + f])
        out.start()
        outs.append(out)

    for f in range(2):
        apply_future_half(0, mc, columns, f)
    take_far(PIV - 1)
    columns = assembled(PIV - 1, other)
    for f in range(2):
        apply_future_half(0, other, columns, f)
        store(f)
    for copy in sent:
        copy.wait_send()
    swap.wait_send()
    for out in outs:
        out.wait()


def deliver(solved_ref, future_ref, solved_out_ref, future_out_ref, solved, future, in_sem, out_sem):
    pairs = [(solved_ref.at[p], solved.at[p], solved_out_ref.at[p]) for p in range(PIV)]
    pairs += [(future_ref.at[f], future.at[f], future_out_ref.at[f]) for f in range(2)]
    arrivals = [pltpu.make_async_copy(a, b, in_sem.at[k]) for k, (a, b, _) in enumerate(pairs)]
    leavings = [pltpu.make_async_copy(b, c, out_sem.at[k]) for k, (_, b, c) in enumerate(pairs)]
    for arrival in arrivals:
        arrival.start()
    for arrival, leaving in zip(arrivals, leavings, strict=True):
        arrival.wait()
        leaving.start()
    for leaving in leavings:
        leaving.wait()


def local(
    pivot_rhs, pivot_inverse, pivot_owner, coupling_left, coupling_right, coupling_ranks,
    future_left, future_right, future_ranks, future_rhs,
):
    hbm = pl.BlockSpec(memory_space=pl.ANY)
    plane, column, ring = len(PLANE), len(COLUMN), len(RING)
    dma = pltpu.SemaphoreType.DMA
    bf16, f32 = jnp.bfloat16, jnp.float32
    solved, future_out = pl.pallas_call(
        kernel,
        out_shape=(
            jax.ShapeDtypeStruct((PIV, PROBES, B), bf16),
            jax.ShapeDtypeStruct(future_rhs.shape, f32),
        ),
        in_specs=[hbm] * 10,
        out_specs=(hbm, hbm),
        scratch_shapes=[
            pltpu.VMEM((B, B), bf16),
            pltpu.VMEM((PROBES, B), f32),
            pltpu.VMEM((PIV - 1, R, B), bf16),
            pltpu.VMEM((PIV - 1, R, B), bf16),
            pltpu.VMEM((NC, *future_left.shape), bf16),
            pltpu.VMEM(future_right.shape, bf16),
            pltpu.VMEM(future_rhs.shape, f32),
            pltpu.VMEM((PIV - 1, R, B), bf16),
            pltpu.VMEM((PROBES, B), f32),
            pltpu.VMEM((PIV, PROBES, B), bf16),
            pltpu.VMEM((PIV - 1, NX, NY, GROUP, COLS), bf16),
            pltpu.VMEM((PIV - 1, plane, GROUP, COLS), bf16),
            pltpu.VMEM((PIV, GROUP, COLS), bf16),
            pltpu.VMEM((PIV, column, GROUP, COLS), bf16),
            pltpu.VMEM((PIV, NC, NX, NY, GROUP, COLS), bf16),
            pltpu.VMEM((NX, NY, RANKS, COLS), bf16),
            pltpu.VMEM((ring, NY, RANKS, COLS), bf16),
            pltpu.VMEM((NY, RANKS, COLS), bf16),
            pltpu.VMEM((ring, RANKS, COLS), bf16),
            pltpu.VMEM((NC, NX, RANKS, COLS), bf16),
            pltpu.VMEM((NX, NY, GROUP, COLS), f32),
            pltpu.VMEM((plane, GROUP, COLS), f32),
            pltpu.VMEM((NX, GROUP, RANKS), f32),
            pltpu.VMEM((ring, NX, GROUP, RANKS), f32),
            pltpu.SMEM(pivot_owner.shape, jnp.int32),
            pltpu.SMEM(coupling_ranks.shape, jnp.int32),
            pltpu.SMEM(future_ranks.shape, jnp.int32),
            dma((3,)),
            dma((6,)),
            dma((B // BLOCK,)),
            dma((PIV + 2,)),
            dma((2,)),
            dma((PIV - 1, plane)),
            dma((PIV - 1, plane)),
            dma((PIV, column)),
            dma((PIV, column)),
            dma((PIV, plane)),
            dma((PIV, plane)),
            dma((PIV, plane + 1)),
            dma((PIV, plane + 1)),
            dma((ring,)),
            dma((ring,)),
            dma((ring,)),
            dma((ring,)),
            dma((ring,)),
            dma((ring,)),
            dma((ring + 1,)),
            dma((ring + 1,)),
            dma((plane,)),
            dma((plane,)),
            dma((ring,)),
            dma((ring,)),
        ],
        compiler_params=pltpu.CompilerParams(collective_id=0, has_side_effects=True),
    )(
        pivot_owner,
        coupling_ranks,
        future_ranks,
        pivot_rhs[0].T,
        pivot_inverse[0],
        coupling_left[0].swapaxes(1, 2),
        coupling_right[0].swapaxes(1, 2),
        future_left,
        future_right,
        future_rhs,
    )
    solved, future_out = pl.pallas_call(
        deliver,
        out_shape=(
            jax.ShapeDtypeStruct(solved.shape, bf16),
            jax.ShapeDtypeStruct(future_out.shape, f32),
        ),
        in_specs=[hbm, hbm],
        out_specs=(hbm, hbm),
        scratch_shapes=[
            pltpu.VMEM(solved.shape, bf16),
            pltpu.VMEM(future_out.shape, f32),
            dma((PIV + 2,)),
            dma((PIV + 2,)),
        ],
    )(solved, future_out)
    return solved.swapaxes(1, 2), future_out


def solution(mesh):
    finer = Mesh(mesh.devices.reshape(NZ, NX, NY, NC), (*TC, "pr"))
    in_specs = (
        P(TC, None, "pr"),
        P(TC, None, None),
        P(),
        P(TC, None, None, None),
        P(TC, None, None, None),
        P(TC, None),
        P(TC, None, None, "pr"),
        P(TC, None, None, "pr"),
        P(TC, None),
        P(TC, None, "pr"),
    )
    out_specs = (P(None, None, "pr"), P(TC, None, "pr"))
    return jax.shard_map(local, mesh=finer, in_specs=in_specs, out_specs=out_specs, check_vma=False)
```

```python
import functools

import jax
import jax.numpy as jnp
from jax import lax
from jax.experimental import pallas as pl
from jax.experimental.pallas import tpu as pltpu
from jax.sharding import Mesh
from jax.sharding import PartitionSpec as P

TC = ("tz", "tx", "ty")
MESH = pl.DeviceIdType.MESH
NZ, NX, NY, NC = 8, 4, 4, 2
PIV, B, PROBES, R = 3, 1536, 32, 200
GROUP, COLS = PROBES // NX, B // NY
RANKS = 56
BLOCK = 256


def ring_distance(step, size):
    return min(step, size - step)


PLANE = sorted(
    ((dx, dy) for dx in range(NX) for dy in range(NY) if (dx, dy) != (0, 0)),
    key=lambda d: -(ring_distance(d[0], NX) + ring_distance(d[1], NY)),
)
COLUMN = sorted(range(1, NZ), key=lambda d: -ring_distance(d, NZ))
RING = (2, 1, 3)


def matmul(a, b):
    return lax.dot_general(a, b, (((1,), (0,)), ((), ())), preferred_element_type=jnp.float32)


def matmul_t(a, b):
    return lax.dot_general(a, b, (((1,), (1,)), ((), ())), preferred_element_type=jnp.float32)


def kernel(
    owner_in, coupling_ranks_in, future_ranks_in,
    rhs_ref, inverse_ref, left_ref, right_ref, future_left_ref, future_right_ref, future_rhs_ref,
    solved_ref, future_out_ref,
    inverse, rhs, left, right, future_left, future_right, future, gain, acc, block,
    rs_send, rs_recv, z_send, z_recv, whole,
    pair_send, pair_recv, pair_mid, pair_last, pair, rest_send, rest_recv, f_send, f_recv,
    owner_ref, coupling_ranks_ref, future_ranks_ref, table_sem,
    load_sem, panel_sem, out_sem, swap_sem,
    rs_send_sem, rs_recv_sem, z_send_sem, z_recv_sem,
    own_send_sem, own_recv_sem, far_send_sem, far_recv_sem,
    pair_send_sem, pair_recv_sem, mid_send_sem, mid_recv_sem, near_send_sem, near_recv_sem, cross_send_sem, cross_recv_sem,
    rest_send_sem, rest_recv_sem, f_send_sem, f_recv_sem,
):
    mz, mx, my, mc = (lax.axis_index(name) for name in (*TC, "pr"))
    me = (mz * NX + mx) * NY + my
    other = 1 - mc

    def shifted(dx, dy):
        return lax.rem(mx + dx, NX), lax.rem(my + dy, NY)

    barrier = pltpu.get_barrier_semaphore()
    greeted = 0
    for dz in COLUMN:
        pz = lax.rem(mz + dz, NZ)
        pl.semaphore_signal(barrier, 1, device_id=(pz, mx, my, mc), device_id_type=MESH)
        greeted += 1
    for dx, dy in PLANE:
        px, py = shifted(dx, dy)
        for core in (mc, other):
            pl.semaphore_signal(barrier, 1, device_id=(mz, px, py, core), device_id_type=MESH)
            greeted += 1
    pl.semaphore_signal(barrier, 1, device_id=(mz, mx, my, other), device_id_type=MESH)
    greeted += 1

    rhs_load = pltpu.make_async_copy(rhs_ref, rhs, load_sem.at[0])
    rhs_load.start()
    panels = []
    for k in range(B // BLOCK):
        rows, columns = pl.ds(k * BLOCK, BLOCK), pl.ds(0, (k + 1) * BLOCK)
        panel = pltpu.make_async_copy(
            inverse_ref.at[rows, columns], inverse.at[rows, columns], panel_sem.at[k]
        )
        panel.start()
        panels.append(panel)

    tables = [
        pltpu.make_async_copy(owner_in, owner_ref, table_sem.at[0]),
        pltpu.make_async_copy(coupling_ranks_in, coupling_ranks_ref, table_sem.at[1]),
        pltpu.make_async_copy(future_ranks_in, future_ranks_ref, table_sem.at[2]),
    ]
    for table in tables:
        table.start()

    loads = [
        pltpu.make_async_copy(right_ref, right, load_sem.at[1]),
        pltpu.make_async_copy(left_ref, left, load_sem.at[2]),
        pltpu.make_async_copy(future_left_ref, future_left.at[mc], load_sem.at[3]),
        pltpu.make_async_copy(future_right_ref, future_right, load_sem.at[4]),
        pltpu.make_async_copy(future_rhs_ref, future, load_sem.at[5]),
    ]

    for load in loads[:2]:
        load.start()
    rhs_load.wait()
    start = rhs[...].astype(jnp.bfloat16)
    sums = [None] * (B // BLOCK)
    for k in range(B // BLOCK):
        panels[k].wait()
        piece = start[:, k * BLOCK : (k + 1) * BLOCK]
        for c in range(k + 1):
            term = matmul(piece, inverse[k * BLOCK : (k + 1) * BLOCK, c * BLOCK : (c + 1) * BLOCK])
            sums[c] = term if sums[c] is None else sums[c] + term
    for c in range(B // BLOCK):
        acc[:, c * BLOCK : (c + 1) * BLOCK] = sums[c]
    for load in loads[2:]:
        load.start()
    pl.semaphore_wait(barrier, greeted)

    swap = pltpu.make_async_remote_copy(
        src_ref=future_left_ref,
        dst_ref=future_left.at[mc],
        send_sem=swap_sem.at[0],
        recv_sem=swap_sem.at[1],
        device_id=(mz, mx, my, other),
        device_id_type=MESH,
    )
    swap_in = pltpu.make_async_remote_copy(
        src_ref=future_left_ref,
        dst_ref=future_left.at[other],
        send_sem=swap_sem.at[0],
        recv_sem=swap_sem.at[1],
        device_id=(mz, mx, my, other),
        device_id_type=MESH,
    )

    for table in tables:
        table.wait()
    own_pivot = jnp.int32(0)
    holds = jnp.int32(0)
    for p in range(PIV):
        mine = (owner_ref[p] == me).astype(jnp.int32)
        own_pivot = own_pivot + mine * p
        holds = holds + mine
    rank_ids = lax.broadcasted_iota(jnp.int32, (PROBES, R), 1)
    future_rank_ids = lax.broadcasted_iota(jnp.int32, (NC * PROBES, R), 1)

    sent = []

    def send(src, dst, send_sem, recv_sem, device):
        copy = pltpu.make_async_remote_copy(
            src_ref=src, dst_ref=dst, send_sem=send_sem, recv_sem=recv_sem,
            device_id=device, device_id_type=MESH,
        )
        copy.start()
        sent.append(copy)

    def receive(dst, send_sem, recv_sem):
        pltpu.make_async_remote_copy(
            src_ref=dst, dst_ref=dst, send_sem=send_sem, recv_sem=recv_sem,
            device_id=(mz, mx, my, other), device_id_type=MESH,
        ).wait_recv()

    def assembled(i, core):
        columns = [
            whole[i, core, :, g].astype(jnp.float32).reshape(PROBES, COLS) for g in range(NY)
        ]
        return jnp.concatenate(columns, axis=1).astype(jnp.bfloat16)

    def make_gain(j):
        for c in range(B // BLOCK):
            columns = pl.ds(c * BLOCK, BLOCK)
            below = pl.ds(c * BLOCK, B - c * BLOCK)
            gain[j, :, columns] = matmul(right[j, :, below], inverse[below, columns]).astype(jnp.bfloat16)

    first, second = mx + mc * (my - mx), my + mc * (mx - my)

    def along_first(d):
        return mz, lax.rem(mx + d * other, NX), lax.rem(my + d * mc, NY), mc

    def along_second(d):
        return mz, lax.rem(mx + d * mc, NX), lax.rem(my + d * other, NY), mc

    def make_pair():
        limit = jnp.where(owner_ref[0] == me, coupling_ranks_ref[0, 0], 0)

        def factor_slice(ref, x, y, count):
            return ref[0, pl.ds(x * RANKS, count), pl.ds(y * COLS, COLS)].astype(jnp.float32)

        for a in range(NX):
            for b in range(NY):
                row, col = min(RANKS, R - a * RANKS), min(RANKS, R - b * RANKS)
                ids = lax.broadcasted_iota(jnp.int32, (RANKS, COLS), 0)
                left_part = factor_slice(left, a, b, row)
                right_part = factor_slice(gain, b, a, col)
                if row < RANKS:
                    left_part = jnp.concatenate([left_part, jnp.zeros((RANKS - row, COLS), jnp.float32)])
                if col < RANKS:
                    right_part = jnp.concatenate([right_part, jnp.zeros((RANKS - col, COLS), jnp.float32)])
                value = jnp.where(mc == 0, left_part, right_part)
                start = (a + mc * (b - a)) * RANKS
                pair_send[a, b] = jnp.where(ids + start < limit, value, 0.0).astype(jnp.bfloat16)

    def spread_pair():
        for k, d in enumerate(RING):
            to = lax.rem(first + d, NX)
            send(pair_send.at[to], pair_recv.at[k], pair_send_sem.at[k], pair_recv_sem.at[k], along_first(d))

    def spread_on():
        for k in range(len(RING)):
            receive(pair_recv.at[k], pair_send_sem.at[k], pair_recv_sem.at[k])
        total = pair_send[first].astype(jnp.float32)
        for k in range(len(RING)):
            total = total + pair_recv[k].astype(jnp.float32)
        pair_mid[...] = total.astype(jnp.bfloat16)
        for k, d in enumerate(RING):
            to = lax.rem(second + d, NY)
            send(pair_mid.at[to], pair_last.at[k], mid_send_sem.at[k], mid_recv_sem.at[k], along_second(d))

    def share_pair():
        total = pair_mid[second].astype(jnp.float32)
        for k in range(len(RING)):
            receive(pair_last.at[k], mid_send_sem.at[k], mid_recv_sem.at[k])
            total = total + pair_last[k].astype(jnp.float32)
        pair[mc, mx] = total.astype(jnp.bfloat16)
        piece = pair.at[mc, mx]
        for k, d in enumerate(RING):
            px = lax.rem(mx + d, NX)
            send(piece, piece, near_send_sem.at[k], near_recv_sem.at[k], (mz, px, my, mc))
            send(piece, piece, cross_send_sem.at[k], cross_recv_sem.at[k], (mz, px, my, other))
        last = len(RING)
        send(piece, piece, cross_send_sem.at[last], cross_recv_sem.at[last], (mz, mx, my, other))

    def take_pair():
        for k, d in enumerate(RING):
            px = lax.rem(mx + NX - d, NX)
            receive(pair.at[mc, px], near_send_sem.at[k], near_recv_sem.at[k])
            receive(pair.at[other, px], cross_send_sem.at[k], cross_recv_sem.at[k])
        last = len(RING)
        receive(pair.at[other, mx], cross_send_sem.at[last], cross_recv_sem.at[last])

    def take_far(i):
        for k, (dx, dy) in enumerate(PLANE):
            px, py = shifted(NX - dx, NY - dy)
            receive(whole.at[i, other, px, py], far_send_sem.at[i, k], far_recv_sem.at[i, k])
        receive(whole.at[i, other, mx, my], far_send_sem.at[i, len(PLANE)], far_recv_sem.at[i, len(PLANE)])

    half = B // NC

    def weighted(probes, f, p, ids):
        weights = matmul_t(probes[:, :half], future_left[0, f, p]) + matmul_t(
            probes[:, half:], future_left[1, f, p]
        )
        weights = jnp.where(ids < future_ranks_ref[f, p], weights, 0.0)
        return matmul(weights.astype(jnp.bfloat16), future_right[f, p])

    def apply_future(i, p):
        take_far(i)
        both = jnp.concatenate([assembled(i, 0), assembled(i, 1)], axis=0)
        for f in range(2):
            future[f] = future[f] - weighted(both, f, p, future_rank_ids)

    def apply_future_half(p, core, probes, f):
        rows = pl.ds(pl.multiple_of(core * PROBES, PROBES), PROBES)
        future[f, rows] = future[f, rows] - weighted(probes, f, p, rank_ids)

    def scatter(i, p):
        masked = jnp.where(owner_ref[p] == me, acc[...], 0.0).reshape(NX, GROUP, B).astype(jnp.bfloat16)
        for g in range(NY):
            rs_send[i, :, g] = masked[:, :, g * COLS : (g + 1) * COLS]
        for k, (dx, dy) in enumerate(PLANE):
            px, py = shifted(dx, dy)
            send(
                rs_send.at[i, px, py], rs_recv.at[i, k],
                rs_send_sem.at[i, k], rs_recv_sem.at[i, k], (mz, px, py, mc),
            )

    def scattered(i):
        part = rs_send[i, mx, my].astype(jnp.float32)
        for k in range(len(PLANE)):
            receive(rs_recv.at[i, k], rs_send_sem.at[i, k], rs_recv_sem.at[i, k])
            part = part + rs_recv[i, k].astype(jnp.float32)
        return part

    def send_column(i, part):
        z_send[i] = part.astype(jnp.bfloat16)
        for k, dz in enumerate(COLUMN):
            send(
                z_send.at[i], z_recv.at[i, k], z_send_sem.at[i, k], z_recv_sem.at[i, k],
                (lax.rem(mz + dz, NZ), mx, my, mc),
            )

    def column_sum(i, part):
        for k in range(len(COLUMN)):
            receive(z_recv.at[i, k], z_send_sem.at[i, k], z_recv_sem.at[i, k])
            part = part + z_recv[i, k].astype(jnp.float32)
        part = part.astype(jnp.bfloat16)
        whole[i, mc, mx, my] = part
        return part

    def gather(i):
        piece = whole.at[i, mc, mx, my]
        for k, (dx, dy) in enumerate(PLANE):
            px, py = shifted(dx, dy)
            send(piece, piece, own_send_sem.at[i, k], own_recv_sem.at[i, k], (mz, px, py, mc))
    def gather_far(i):
        piece = whole.at[i, mc, mx, my]
        for k, (dx, dy) in enumerate(PLANE):
            px, py = shifted(dx, dy)
            send(piece, piece, far_send_sem.at[i, k], far_recv_sem.at[i, k], (mz, px, py, other))
        last = len(PLANE)
        send(piece, piece, far_send_sem.at[i, last], far_recv_sem.at[i, last], (mz, mx, my, other))

    def gather_both(i):
        piece = whole.at[i, mc, mx, my]
        for k, (dx, dy) in enumerate(PLANE):
            px, py = shifted(dx, dy)
            send(piece, piece, own_send_sem.at[i, k], own_recv_sem.at[i, k], (mz, px, py, mc))
            send(piece, piece, far_send_sem.at[i, k], far_recv_sem.at[i, k], (mz, px, py, other))
        last = len(PLANE)
        send(piece, piece, far_send_sem.at[i, last], far_recv_sem.at[i, last], (mz, mx, my, other))

    outs = []

    def gathered(i, p):
        for k, (dx, dy) in enumerate(PLANE):
            px, py = shifted(NX - dx, NY - dy)
            receive(whole.at[i, mc, px, py], own_send_sem.at[i, k], own_recv_sem.at[i, k])
        columns = assembled(i, mc)
        block[i] = columns
        out = pltpu.make_async_copy(block.at[i], solved_ref.at[p], out_sem.at[i])
        out.start()
        outs.append(out)
        return columns

    scatter(0, 2)
    loads[0].wait()
    loads[1].wait()
    make_gain(0)
    make_pair()
    spread_pair()
    swap.start()
    part = scattered(0)
    send_column(0, part)
    make_gain(1)
    column_sum(0, part)
    gather(0)
    spread_on()
    columns = gathered(0, 2)
    entry = jnp.clip(2 - own_pivot - 1, 0, PIV - 2)
    active = holds * (own_pivot < 2).astype(jnp.int32)
    factor = matmul_t(columns, left[entry])
    factor = jnp.where(rank_ids < coupling_ranks_ref[0, entry] * active, factor, 0.0)
    acc[...] = acc[...] - matmul(factor.astype(jnp.bfloat16), gain[entry])

    scatter(1, 1)
    share_pair()
    part = scattered(1)
    send_column(1, part)
    rest = jnp.where(owner_ref[0] == me, acc[...], 0.0).reshape(NX, GROUP, B)
    for g in range(NY):
        rest_send[:, g] = rest[:, :, g * COLS : (g + 1) * COLS]
    for k, (dx, dy) in enumerate(PLANE):
        px, py = shifted(dx, dy)
        send(
            rest_send.at[px, py], rest_recv.at[k], rest_send_sem.at[k], rest_recv_sem.at[k],
            (mz, px, py, mc),
        )
    gather_far(0)
    swap_in.wait_recv()
    for load in loads[2:]:
        load.wait()
    slice_1 = column_sum(1, part)

    take_pair()
    for x in range(NX):
        f_send[x] = matmul_t(slice_1, pair[0, x])
    for k, d in enumerate(RING):
        send(
            f_send, f_recv.at[k], f_send_sem.at[k], f_recv_sem.at[k],
            (mz, mx, lax.rem(my + d, NY), mc),
        )
    gather(1)
    gather_far(1)
    part = rest_send[mx, my]
    for k in range(len(PLANE)):
        receive(rest_recv.at[k], rest_send_sem.at[k], rest_recv_sem.at[k])
        part = part + rest_recv[k]
    for k in range(len(RING)):
        receive(f_recv.at[k], f_send_sem.at[k], f_recv_sem.at[k])
    for x in range(NX):
        factor = f_send[x]
        for k in range(len(RING)):
            factor = factor + f_recv[k, x]
        part = part - matmul(factor.astype(jnp.bfloat16), pair[1, x])
    send_column(2, part)
    gathered(1, 1)
    apply_future(0, 2)
    apply_future(1, 1)
    column_sum(2, part)
    gather_both(2)
    columns = gathered(2, 0)

    def store(f):
        out = pltpu.make_async_copy(future.at[f], future_out_ref.at[f], out_sem.at[PIV + f])
        out.start()
        outs.append(out)

    for f in range(2):
        apply_future_half(0, mc, columns, f)
    take_far(PIV - 1)
    columns = assembled(PIV - 1, other)
    for f in range(2):
        apply_future_half(0, other, columns, f)
        store(f)
    for copy in sent:
        copy.wait_send()
    swap.wait_send()
    for out in outs:
        out.wait()


def deliver(solved_ref, future_ref, solved_out_ref, future_out_ref, solved, future, in_sem, out_sem):
    pairs = [(solved_ref.at[p], solved.at[p], solved_out_ref.at[p]) for p in range(PIV)]
    pairs += [(future_ref.at[f], future.at[f], future_out_ref.at[f]) for f in range(2)]
    arrivals = [pltpu.make_async_copy(a, b, in_sem.at[k]) for k, (a, b, _) in enumerate(pairs)]
    leavings = [pltpu.make_async_copy(b, c, out_sem.at[k]) for k, (_, b, c) in enumerate(pairs)]
    for arrival in arrivals:
        arrival.start()
    for arrival, leaving in zip(arrivals, leavings, strict=True):
        arrival.wait()
        leaving.start()
    for leaving in leavings:
        leaving.wait()


def local(
    pivot_rhs, pivot_inverse, pivot_owner, coupling_left, coupling_right, coupling_ranks,
    future_left, future_right, future_ranks, future_rhs,
):
    hbm = pl.BlockSpec(memory_space=pl.ANY)
    plane, column, ring = len(PLANE), len(COLUMN), len(RING)
    dma = pltpu.SemaphoreType.DMA
    bf16, f32 = jnp.bfloat16, jnp.float32
    solved, future_out = pl.pallas_call(
        kernel,
        out_shape=(
            jax.ShapeDtypeStruct((PIV, PROBES, B), bf16),
            jax.ShapeDtypeStruct(future_rhs.shape, f32),
        ),
        in_specs=[hbm] * 10,
        out_specs=(hbm, hbm),
        scratch_shapes=[
            pltpu.VMEM((B, B), bf16),
            pltpu.VMEM((PROBES, B), f32),
            pltpu.VMEM((PIV - 1, R, B), bf16),
            pltpu.VMEM((PIV - 1, R, B), bf16),
            pltpu.VMEM((NC, *future_left.shape), bf16),
            pltpu.VMEM(future_right.shape, bf16),
            pltpu.VMEM(future_rhs.shape, f32),
            pltpu.VMEM((PIV - 1, R, B), bf16),
            pltpu.VMEM((PROBES, B), f32),
            pltpu.VMEM((PIV, PROBES, B), bf16),
            pltpu.VMEM((PIV - 1, NX, NY, GROUP, COLS), bf16),
            pltpu.VMEM((PIV - 1, plane, GROUP, COLS), bf16),
            pltpu.VMEM((PIV, GROUP, COLS), bf16),
            pltpu.VMEM((PIV, column, GROUP, COLS), bf16),
            pltpu.VMEM((PIV, NC, NX, NY, GROUP, COLS), bf16),
            pltpu.VMEM((NX, NY, RANKS, COLS), bf16),
            pltpu.VMEM((ring, NY, RANKS, COLS), bf16),
            pltpu.VMEM((NY, RANKS, COLS), bf16),
            pltpu.VMEM((ring, RANKS, COLS), bf16),
            pltpu.VMEM((NC, NX, RANKS, COLS), bf16),
            pltpu.VMEM((NX, NY, GROUP, COLS), f32),
            pltpu.VMEM((plane, GROUP, COLS), f32),
            pltpu.VMEM((NX, GROUP, RANKS), f32),
            pltpu.VMEM((ring, NX, GROUP, RANKS), f32),
            pltpu.SMEM(pivot_owner.shape, jnp.int32),
            pltpu.SMEM(coupling_ranks.shape, jnp.int32),
            pltpu.SMEM(future_ranks.shape, jnp.int32),
            dma((3,)),
            dma((6,)),
            dma((B // BLOCK,)),
            dma((PIV + 2,)),
            dma((2,)),
            dma((PIV - 1, plane)),
            dma((PIV - 1, plane)),
            dma((PIV, column)),
            dma((PIV, column)),
            dma((PIV, plane)),
            dma((PIV, plane)),
            dma((PIV, plane + 1)),
            dma((PIV, plane + 1)),
            dma((ring,)),
            dma((ring,)),
            dma((ring,)),
            dma((ring,)),
            dma((ring,)),
            dma((ring,)),
            dma((ring + 1,)),
            dma((ring + 1,)),
            dma((plane,)),
            dma((plane,)),
            dma((ring,)),
            dma((ring,)),
        ],
        compiler_params=pltpu.CompilerParams(collective_id=0, has_side_effects=True),
    )(
        pivot_owner,
        coupling_ranks,
        future_ranks,
        pivot_rhs[0].T,
        pivot_inverse[0],
        coupling_left[0].swapaxes(1, 2),
        coupling_right[0].swapaxes(1, 2),
        future_left,
        future_right,
        future_rhs,
    )
    solved, future_out = pl.pallas_call(
        deliver,
        out_shape=(
            jax.ShapeDtypeStruct(solved.shape, bf16),
            jax.ShapeDtypeStruct(future_out.shape, f32),
        ),
        in_specs=[hbm, hbm],
        out_specs=(hbm, hbm),
        scratch_shapes=[
            pltpu.VMEM(solved.shape, bf16),
            pltpu.VMEM(future_out.shape, f32),
            dma((PIV + 2,)),
            dma((PIV + 2,)),
        ],
    )(solved, future_out)
    return solved.swapaxes(1, 2), future_out


def solution(mesh):
    finer = Mesh(mesh.devices.reshape(NZ, NX, NY, NC), (*TC, "pr"))
    in_specs = (
        P(TC, None, "pr"),
        P(TC, None, None),
        P(),
        P(TC, None, None, None),
        P(TC, None, None, None),
        P(TC, None),
        P(TC, None, None, "pr"),
        P(TC, None, None, "pr"),
        P(TC, None),
        P(TC, None, "pr"),
    )
    out_specs = (P(None, None, "pr"), P(TC, None, "pr"))
    return jax.shard_map(local, mesh=finer, in_specs=in_specs, out_specs=out_specs, check_vma=False)
```
